256 devices in a mesh: leaf: 64 (over z, y, core), cols: 4 (over x).
Axes of the slice: x: 4, y: 4, z: 8, core: 2. Of those that a mesh axis runs over, the one named last changes fastest.
Arguments:
- points: bfloat16 [262144, 64], P('leaf', 'cols'), may hold values from -6 to 6
- weights: bfloat16 [262144, 1024], P('leaf', 'cols'), may hold values from -6 to 6
- leaf_basis: bfloat16 [65536, 1024], P('leaf'), may hold values from -0.1875 to 0.1875
- dev_transfer: bfloat16 [16384, 1024], P('leaf'), may hold values from -0.1875 to 0.1875
- group_transfer: bfloat16 [4096, 1024], P('leaf'), may hold values from -0.1875 to 0.1875
- leaf_skeleton: int32 [256, 256], P('leaf'), may hold values from 0 to 1023, as said below
- dev_skeleton: int32 [64, 256], P('leaf'), may hold values from 0 to 1023, as said below
- group_skeleton: int32 [16, 256], replicated, may hold values from 0 to 1023, as said below
- near_list: int32 [256, 3], P('leaf'), may hold values from 0 to 255, as said below
- near_count: int32 [256], P('leaf'), may hold values from 1 to 3
Outputs:
- potentials: float32 [262144, 1024], P('leaf', 'cols')
The draws below stay inside these ranges and needn't reach their ends.
Inputs may be any that keep to these rules, and one draw needn't show every extreme that they name: `leaf_skeleton`: each row holds 256 distinct point numbers within the leaf. `dev_skeleton`: each row holds 256 distinct numbers into the 1024 skeleton points of the node's children, in child order. `group_skeleton`: each row holds 256 distinct numbers into the 1024 skeleton points of the node's children, in child order. `near_list`: row l names leaves of the first-level node holding leaf l and of the first-level nodes just before and after it; its first entry is l itself and its first near_count[l] entries are distinct; later entries are leaf numbers that are not used.
All inputs are finite; a program needn't handle non-finite values.
Results may differ from the reference program's by a relative error of at most 0.005.
Values may be sent and summed in bfloat16 or wider, within the bound.
No kernel may reach another device: no remote copies, remote signals or barrier semaphores. Data moves between devices by JAX's collectives and lax.ppermute only.
A program may use at most 128 MiB of HBM per device.

```python
import jax
import jax.numpy as jnp
from jax import lax

DIM = 64
COLS = 1024
RANK = 256
LEAF = 1024
LD = 4
NEARMAX = 3
LEAVES = 256
NPTS = 262144
GROUPS = 16
N_LEAF = 64


def pick_rows(key, row_count, choices_of, kept):
    scores = jax.random.randint(key, (row_count, choices_of), 0, 1 << 20) * choices_of + jnp.arange(choices_of, dtype=jnp.int32)[None, :]
    ordering = jnp.argsort(scores, axis=1, stable=True)
    return ordering[:, :kept].astype(jnp.int32)


def draw_leaf_skeleton(key, part):
    return pick_rows(jax.random.fold_in(key, 11), LD * N_LEAF, LEAF, RANK)


def draw_dev_skeleton(key, part):
    return pick_rows(jax.random.fold_in(key, 12), N_LEAF, LD * RANK, RANK)


def draw_group_skeleton(key, part):
    return pick_rows(jax.random.fold_in(key, 13), N_LEAF // LD, LD * RANK, RANK)


def near_tables(key):
    leaves = LD * N_LEAF
    key_order, key_count = jax.random.split(jax.random.fold_in(key, 21))
    leaf_ids = jnp.arange(leaves, dtype=jnp.int32)
    block_ids = leaf_ids // LD
    slot_ids = leaf_ids % LD
    offsets = jnp.arange(3 * LD, dtype=jnp.int32)
    candidates = (block_ids[:, None] - 1) * LD + offsets[None, :]
    valid_mask = (candidates >= 0) & (candidates < leaves) & (candidates != leaf_ids[:, None])
    forced_pick = (slot_ids[:, None] == LD - 1) & (candidates == (block_ids[:, None] + 1) * LD) | (slot_ids[:, None] == 0) & (candidates == block_ids[:, None] * LD - 1)
    forced_pick = forced_pick & valid_mask
    scores = jax.random.randint(key_order, (leaves, 3 * LD), 0, 1 << 16) * (4 * LD) + offsets[None, :]
    scores = jnp.where(valid_mask, scores, scores + (1 << 24))
    scores = jnp.where(forced_pick, -1, scores)
    ordering = jnp.argsort(scores, axis=1, stable=True)
    chosen = jnp.take_along_axis(candidates, ordering, axis=1)[:, :NEARMAX - 1]
    near_table = jnp.concatenate([leaf_ids[:, None], chosen], axis=1).astype(jnp.int32)
    near_len = jax.random.randint(key_count, (leaves,), 1, NEARMAX + 1)
    near_len = jnp.where(jnp.any(forced_pick, axis=1), jnp.maximum(near_len, 2), near_len)
    near_len = jnp.where(leaf_ids == 1, NEARMAX, near_len)
    near_len = jnp.where(leaf_ids == 2, 1, near_len)
    return (near_table, near_len.astype(jnp.int32))


def draw_near_list(key, part):
    return near_tables(key)[0]


def draw_near_count(key, part):
    return near_tables(key)[1]


def levels(own_key, dims, shards, low, high):
    factor_of = 1.0
    for dim, blocks in shards:
        steps = jax.random.uniform(jax.random.fold_in(jax.random.fold_in(own_key, 6), dim), (blocks,), jnp.float32, low / len(shards), high / len(shards))
        factor_of = factor_of * jnp.repeat(jnp.exp(steps), dims[dim] // blocks).reshape((-1,) + (1,) * (len(dims) - 1 - dim))
    return factor_of


def gaussian(own_key, shape, spread, bound, pieces=(), kind=jnp.bfloat16):
    values = spread * jax.random.normal(own_key, shape, jnp.float32)
    if pieces:
        values = values * levels(own_key, shape, pieces, -0.22, 0.18)
    return jnp.clip(values, -bound, bound).astype(kind)


def setup_inputs(seed: int = 0) -> dict:
    key_of = jax.random.split(jax.random.key(seed), 11)
    points = gaussian(key_of[0], (NPTS, DIM), 1.0, 6.0, ((0, 64), (1, 4)))
    weights = gaussian(key_of[1], (NPTS, COLS), 1.0, 6.0, ((0, 64), (1, 4)))
    leaf_basis = gaussian(key_of[2], (LEAVES * RANK, LEAF), LEAF ** -0.5, 0.1875, ((0, 64),))
    dev_transfer = gaussian(key_of[3], (N_LEAF * RANK, LD * RANK), (LD * RANK) ** -0.5, 0.1875, ((0, 64),))
    group_transfer = gaussian(key_of[4], (GROUPS * RANK, LD * RANK), (LD * RANK) ** -0.5, 0.1875, ((0, 64),))
    leaf_skeleton = draw_leaf_skeleton(jax.random.fold_in(key_of[10], 71), 0)
    dev_skeleton = draw_dev_skeleton(jax.random.fold_in(key_of[10], 71), 0)
    group_skeleton = draw_group_skeleton(jax.random.fold_in(key_of[10], 71), 0)
    near_list = draw_near_list(jax.random.fold_in(key_of[10], 71), 0)
    near_count = draw_near_count(jax.random.fold_in(key_of[10], 71), 0)
    return {"points": points, "weights": weights, "leaf_basis": leaf_basis, "dev_transfer": dev_transfer, "group_transfer": group_transfer, "leaf_skeleton": leaf_skeleton, "dev_skeleton": dev_skeleton, "group_skeleton": group_skeleton, "near_list": near_list, "near_count": near_count}


SHARPNESS = 2.0


def product(left_side, right_side):
    return jnp.dot(left_side.astype(jnp.float32), right_side.astype(jnp.float32), precision=lax.Precision.HIGHEST)


def kernel_matrix(row_points, col_points):
    row_float = row_points.astype(jnp.float32)
    col_float = col_points.astype(jnp.float32)
    inner_prod = jnp.dot(row_float, col_float.T, precision=lax.Precision.HIGHEST)
    row_norms = jnp.sum(row_float * row_float, axis=1)
    col_norms = jnp.sum(col_float * col_float, axis=1)
    return jnp.exp((-SHARPNESS / row_points.shape[1]) * (row_norms[:, None] + col_norms[None, :] - 2.0 * inner_prod))


def sibling_term(coords, skeleton_vals, skel_rank):
    blocks = jnp.arange(coords.shape[0], dtype=jnp.int32) // skel_rank
    coupling = jnp.where(blocks[:, None] != blocks[None, :], kernel_matrix(coords, coords), 0.0).astype(jnp.bfloat16)
    return product(coupling, skeleton_vals)


def reference(points, weights, leaf_basis, dev_transfer, group_transfer, leaf_skeleton, dev_skeleton, group_skeleton, near_list, near_count):
    leaves = LD * N_LEAF
    groups = N_LEAF // LD
    leaf_points = points.reshape(leaves, LEAF, DIM)
    leaf_weights = weights.reshape(leaves, LEAF, COLS)
    leaf_maps = leaf_basis.reshape(leaves, RANK, LEAF)
    leaf_skel = jnp.einsum('lrp,lpc->lrc', leaf_maps.astype(jnp.float32), leaf_weights.astype(jnp.float32), precision=lax.Precision.HIGHEST).astype(jnp.bfloat16)
    leaf_coords = jnp.take_along_axis(leaf_points, leaf_skeleton[:, :, None], axis=1)

    def node_level(items):
        skeleton_vals, coords, transfer, chosen = items
        field = sibling_term(coords, skeleton_vals, RANK)
        return field, product(transfer, skeleton_vals).astype(jnp.bfloat16), jnp.take(coords, chosen, axis=0)

    leaf_field, node_skel, node_coords = lax.map(node_level, (leaf_skel.reshape(N_LEAF, LD * RANK, COLS), leaf_coords.reshape(N_LEAF, LD * RANK, DIM), dev_transfer.reshape(N_LEAF, RANK, LD * RANK), dev_skeleton))
    node_field, group_skel, group_coords = lax.map(node_level, (node_skel.reshape(groups, LD * RANK, COLS), node_coords.reshape(groups, LD * RANK, DIM), group_transfer.reshape(groups, RANK, LD * RANK), group_skeleton))
    top_field = sibling_term(group_coords.reshape(groups * RANK, DIM), group_skel.reshape(groups * RANK, COLS), RANK).astype(jnp.bfloat16)
    node_down = jnp.einsum('grk,grc->gkc', group_transfer.reshape(groups, RANK, LD * RANK).astype(jnp.float32), top_field.reshape(groups, RANK, COLS).astype(jnp.float32), precision=lax.Precision.HIGHEST)
    node_total = (node_field + node_down).astype(jnp.bfloat16)
    leaf_down = jnp.einsum('drk,drc->dkc', dev_transfer.reshape(N_LEAF, RANK, LD * RANK).astype(jnp.float32), node_total.reshape(N_LEAF, RANK, COLS).astype(jnp.float32), precision=lax.Precision.HIGHEST)
    leaf_total = (leaf_field + leaf_down).astype(jnp.bfloat16).reshape(leaves, RANK, COLS)

    def finish(items):
        leaf_no, leaf_map, field, near_row, near_len = items
        far_part = product(leaf_map.T, field)
        near_sum = jnp.zeros((LEAF, COLS), jnp.float32)
        for slot_no in range(NEARMAX):
            def add_tile(source):
                block = kernel_matrix(leaf_points[leaf_no], leaf_points[source]).astype(jnp.bfloat16)
                return product(block, leaf_weights[source])

            def no_tile(source):
                return jnp.zeros((LEAF, COLS), jnp.float32)

            near_sum = near_sum + lax.cond(slot_no < near_len, add_tile, no_tile, near_row[slot_no])
        return near_sum + far_part

    result = lax.map(finish, (jnp.arange(leaves, dtype=jnp.int32), leaf_maps, leaf_total, near_list, near_count))
    return result.reshape(leaves * LEAF, COLS)
```

```python
import jax
import jax.numpy as jnp
from jax import lax
from jax.experimental import pallas as pl
from jax.experimental.pallas import tpu as pltpu
from jax.sharding import PartitionSpec as P

LEAF = 1024
RANK = 256
SHARPNESS = 2.0
LOG2E = 1.4426950408889634
BF = jnp.bfloat16
F32 = jnp.float32

VMEM = pl.BlockSpec(memory_space=pltpu.VMEM)
SMEM = pl.BlockSpec(memory_space=pltpu.SMEM)


def mm(a, b):
    return lax.dot_general(a, b, (((1,), (0,)), ((), ())), preferred_element_type=F32)


def mm_nt(a, b):
    return lax.dot_general(a, b, (((1,), (1,)), ((), ())), preferred_element_type=F32)


def mm_tn(a, b):
    return lax.dot_general(a, b, (((0,), (0,)), ((), ())), preferred_element_type=F32)


def call(body, outs, in_specs, scratch=(), flops=0, exps=0, nbytes=0, name=None):
    return pl.pallas_call(
        body,
        out_shape=[jax.ShapeDtypeStruct(s, d) for s, d in outs],
        in_specs=in_specs,
        out_specs=[VMEM] * len(outs),
        scratch_shapes=list(scratch),
        cost_estimate=pl.CostEstimate(flops=flops, transcendentals=exps, bytes_accessed=nbytes),
        compiler_params=pltpu.CompilerParams(vmem_limit_bytes=60 * 1024 * 1024),
        name=name,
    )


def one_hot(index_row, rows):
    numbers = lax.broadcasted_iota(jnp.int32, (rows, index_row.shape[1]), 0)
    return jnp.where(numbers == index_row, 1.0, 0.0).astype(BF)


def tails(coords_t):
    wide = coords_t.astype(F32)
    half = -0.5 * jnp.sum(wide * wide, axis=0, keepdims=True)
    high = half.astype(BF).astype(F32)
    rest = half - high
    mid = rest.astype(BF).astype(F32)
    low = rest - mid
    row = lax.broadcasted_iota(jnp.int32, (16, coords_t.shape[1]), 0)

    def pieces(base, ones):
        out = jnp.where((row >= ones) & (row < ones + 3), 1.0, 0.0)
        out = jnp.where(row == base, high, out)
        out = jnp.where(row == base + 1, mid, out)
        return jnp.where(row == base + 2, low, out)

    return pieces(3, 0), pieces(0, 3)


def right_form(coords_t):
    _, tail = tails(coords_t)
    n = coords_t.shape[1]
    return jnp.concatenate([coords_t, tail.astype(BF), jnp.zeros((48, n), BF)], axis=0)


def left_form(coords_t):
    tail, _ = tails(coords_t)
    n = coords_t.shape[1]
    wide = jnp.concatenate([coords_t.astype(F32), tail, jnp.zeros((48, n), F32)], axis=0)
    return wide.T.astype(BF)


def kernel_block(left, right, dim):
    scale = 2.0 * SHARPNESS / dim * LOG2E
    return jnp.exp2(mm(left, right) * scale).astype(BF)


def select_body(place, points, leaf_skeleton, dev_skeleton, group_skeleton, out):
    member, group = place[0], place[1]
    picked = []
    for leaf in range(4):
        hot = one_hot(leaf_skeleton[pl.ds(leaf, 1), :], LEAF)
        picked.append(mm(points[:, leaf * LEAF : (leaf + 1) * LEAF], hot).astype(BF))
    leaf_coords = jnp.concatenate(picked, axis=1)
    node_coords = mm(leaf_coords, one_hot(dev_skeleton[...], 4 * RANK)).astype(BF)
    chosen = group_skeleton[pl.ds(group, 1), :] - member * RANK
    out[0:16, :] = node_coords
    out[16:32, :] = mm(node_coords, one_hot(chosen, RANK)).astype(BF)


def skel_body(place, weights, basis, transfer, leaf_skel, chunks, total):
    step = pl.program_id(0)
    skel = mm(basis[...], weights[...]).astype(BF)
    leaf_skel[...] = skel
    part = mm(transfer[...], skel)

    @pl.when(step == 0)
    def _():
        total[...] = part

    @pl.when(step > 0)
    def _():
        total[...] += part

    @pl.when(step == 3)
    def _():
        total[...] = total[...].T
        for flip in range(4):
            start = pl.multiple_of(place[4 + flip] * 64, 64)
            chunks[pl.ds(flip * 64, 64), :] = total[pl.ds(start, 64), :].astype(BF)


def forms_body(p0, p1, p2, p3, coords, left, right):
    for n, part in enumerate((p0, p1, p2, p3)):
        coords[pl.ds(n * 16, 16), :] = part[...]
    for leaf in range(4):
        cols = slice(leaf * LEAF, (leaf + 1) * LEAF)
        value = coords[:, cols]
        left[cols, :] = left_form(value)
        right[:, cols] = right_form(value)


def leaf_field_body(coords, leaf_skeleton, leaf_skel, field):
    dim = coords.shape[0]
    lefts, rights = [], []
    for leaf in range(4):
        hot = one_hot(leaf_skeleton[pl.ds(leaf, 1), :], LEAF)
        picked = mm(coords[:, leaf * LEAF : (leaf + 1) * LEAF], hot).astype(BF)
        lefts.append(left_form(picked))
        rights.append(right_form(picked))
    for i in range(4):
        total = None
        for j in range(4):
            if i != j:
                part = mm(kernel_block(lefts[i], rights[j], dim), leaf_skel[j * RANK : (j + 1) * RANK, :])
                total = part if total is None else total + part
        field[i * RANK : (i + 1) * RANK, :] = total


def near_tile(out, left, right, weights, leaf, source, first, dim):
    cols = pl.ds(pl.multiple_of(source * LEAF, LEAF), LEAF)
    for chunk in range(4):
        rows = pl.ds(pl.multiple_of(leaf * LEAF + chunk * 256, 256), 256)
        block = kernel_block(left[rows, :], right[:, cols], dim)
        part = mm(block, weights[cols, :])
        if first:
            out[rows, :] = part
        else:
            out[rows, :] += part


def near_own_body(dim, near_list, near_count, place, left, right, weights, out):
    base = place[2] * 4

    def leaf_step(leaf, carry):
        near_tile(out, left, right, weights, leaf, leaf, True, dim)

        def slot_step(slot, carry):
            source = near_list[leaf, slot] - base
            active = (slot < near_count[leaf]) & (source >= 0) & (source < 4)

            @pl.when(active)
            def _():
                near_tile(out, left, right, weights, leaf, source, False, dim)

            return carry

        return lax.fori_loop(1, 3, slot_step, carry)

    lax.fori_loop(0, 4, leaf_step, 0)


def near_far_body(dim, near_list, near_count, place, left, before, after, w_before, w_after, start, out, right):
    base = place[2] * 4
    for leaf in range(4):
        cols = slice(leaf * LEAF, (leaf + 1) * LEAF)
        right[0, :, cols] = right_form(before[:, cols])
        right[1, :, cols] = right_form(after[:, cols])
    out[...] = start[...]

    def leaf_step(leaf, carry):
        def slot_step(slot, carry):
            source = near_list[leaf, slot] - base
            active = slot < near_count[leaf]

            @pl.when(active & (source < 0) & (source >= -4))
            def _():
                near_tile(out, left, right.at[0], w_before, leaf, source + 4, False, dim)

            @pl.when(active & (source >= 4) & (source < 8))
            def _():
                near_tile(out, left, right.at[1], w_after, leaf, source - 4, False, dim)

            return carry

        return lax.fori_loop(1, 3, slot_step, carry)

    lax.fori_loop(0, 4, leaf_step, 0)


def group_body(place, r0, r1, r2, r3, g0, g1, g2, g3, skel, transfer):
    member = place[0]
    for flip, part in enumerate((g0, g1, g2, g3)):
        rows = pl.ds(pl.multiple_of((member ^ flip) * 64, 64), 64)
        transfer[rows, :] = part[...]
    total = None
    for flip, part in enumerate((r0, r1, r2, r3)):
        cols = pl.ds(pl.multiple_of((member ^ flip) * RANK, RANK), RANK)
        value = mm_nt(part[...], transfer[:, cols])
        total = value if total is None else total + value
    skel[...] = total.astype(BF)


def top_body(place, x0, x1, x2, x3, s0, s1, s2, s3, s4, r0, r1, r2, r3, transfer, out, coords):
    member = place[0]
    pieces = (x0, x1, x2, x3)
    dim = 64

    def block_coords(number):
        return jnp.concatenate([piece[number * 16 : (number + 1) * 16, :] for piece in pieces], axis=0)

    own_left = left_form(block_coords(0))
    top = None
    place_of = []
    for ref in (s0, s1, s2, s3, s4):
        place_of += [(ref, row) for row in range(0, ref.shape[0], 64)]
    for number in range(1, 16):
        block = kernel_block(own_left, right_form(block_coords(number)), dim)
        ref, row = place_of[number]
        part = mm_nt(ref[row : row + 64, :], block)
        top = part if top is None else top + part
    top = top.astype(BF)
    nodes = [block_coords(16 + n) for n in range(4)]
    lefts = [left_form(value) for value in nodes]
    rights = [right_form(value) for value in nodes]
    skels = (r0, r1, r2, r3)
    for i in range(4):
        cols = pl.ds(pl.multiple_of((member ^ i) * RANK, RANK), RANK)
        total = mm(top, transfer[:, cols])
        for j in range(4):
            if i != j:
                total = total + mm(skels[j][...], kernel_block(lefts[j], rights[i], dim))
        out[i * 64 : (i + 1) * 64, :] = total.astype(BF)


def finish_body(place, t0, t1, t2, t3, transfer, basis, field, near, out, total):
    for flip, part in enumerate((t0, t1, t2, t3)):
        rows = pl.ds(pl.multiple_of(place[4 + flip] * 64, 64), 64)
        total[rows, :] = part[...].astype(F32)
    node_total = total[...].T.astype(BF)
    leaf_total = (field[...] + mm_tn(transfer[...], node_total)).astype(BF)
    out[...] = near[...] + mm_tn(basis[...], leaf_total)


def per_device(
    points,
    weights,
    leaf_basis,
    dev_transfer,
    group_transfer,
    leaf_skeleton,
    dev_skeleton,
    group_skeleton,
    near_list,
    near_count,
):
    count = lax.axis_size("leaf")
    cols_count = lax.axis_size("cols")
    position = lax.axis_index("leaf")
    member, group = position % 4, position // 4
    share = member ^ (2 * (group % 2))
    place = jnp.stack([member, group, position, position * 0] + [share ^ flip for flip in range(4)]).astype(jnp.int32)
    dim = points.shape[1] * cols_count
    width = weights.shape[1]
    rows = points.shape[0]

    def flipped(value, flip):
        return lax.ppermute(value, "leaf", [(i, i ^ flip) for i in range(count)])

    def across(value):
        return lax.ppermute(value, "leaf", [(i, i // 8 * 8 + (3 - i % 8 // 2) * 2 + i % 2) for i in range(count)])

    def z_step(value, odd):
        pairs = []
        for i in range(count):
            z, rest = i // 8, i % 8
            other = (z ^ 1) if not odd else (((z + 1) ^ 1) - 1) % (count // 8)
            pairs.append((i, other * 8 + rest))
        return lax.ppermute(value, "leaf", pairs)

    def shifted(value, step):
        return lax.ppermute(value, "cols", [(i, (i + step) % cols_count) for i in range(cols_count)])

    def from_all_groups(value):
        pair = jnp.concatenate([value, across(value)], axis=0)
        first = z_step(pair, False)
        second = z_step(jnp.concatenate([pair, first], axis=0), True)
        third = z_step(second, False)
        fourth = z_step(third, True)
        return pair, first, second, third, fourth

    up = [(i, i + 1) for i in range(count - 1)]
    down = [(j, i) for i, j in up]
    shard = points.T
    parts = [shard] + [shifted(shard, step) for step in (1, 2, 3)]
    w_before = lax.ppermute(weights, "leaf", up)
    w_after = lax.ppermute(weights, "leaf", down)
    transfers = [group_transfer] + [flipped(group_transfer, flip) for flip in (1, 2, 3)]

    (picked,) = call(
        select_body,
        [((32, RANK), BF)],
        [SMEM, VMEM, VMEM, VMEM, VMEM],
        flops=2 * 16 * RANK * 5 * LEAF * 8,
        nbytes=rows * 32,
        name="select",
    )(place, shard, leaf_skeleton, dev_skeleton, group_skeleton)
    family = [picked] + [flipped(picked, flip) for flip in (1, 2, 3)]
    node_shards = [value[:16] for value in family]
    group_shard = sum(value[16:].astype(F32) for value in family).astype(BF)
    shard_list = jnp.concatenate(list(from_all_groups(group_shard)) + node_shards, axis=0)
    coord_parts = [shard_list] + [shifted(shard_list, step) for step in (1, 2, 3)]

    leaf_skel, chunks = pl.pallas_call(
        skel_body,
        grid=(4,),
        out_shape=[jax.ShapeDtypeStruct((4 * RANK, width), BF), jax.ShapeDtypeStruct((width, RANK), BF)],
        in_specs=[
            SMEM,
            pl.BlockSpec((LEAF, width), lambda i: (i, 0)),
            pl.BlockSpec((RANK, LEAF), lambda i: (i, 0)),
            pl.BlockSpec((RANK, RANK), lambda i: (0, i)),
        ],
        out_specs=[pl.BlockSpec((RANK, width), lambda i: (i, 0)), pl.BlockSpec((width, RANK), lambda i: (0, 0))],
        scratch_shapes=[pltpu.VMEM((RANK, width), F32)],
        cost_estimate=pl.CostEstimate(
            flops=2 * 5 * RANK * LEAF * width, transcendentals=0, bytes_accessed=5 * 1024 * 1024
        ),
        name="skel",
    )(place, weights, leaf_basis, dev_transfer)
    skels = [chunks[:64]] + [flipped(chunks[flip * 64 : (flip + 1) * 64], flip) for flip in (1, 2, 3)]

    group_skel, full_transfer = call(
        group_body,
        [((64, RANK), BF), ((RANK, 4 * RANK), BF)],
        [SMEM] + [VMEM] * 8,
        flops=2 * 64 * RANK * LEAF * 4,
        nbytes=1024 * 1024,
        name="group",
    )(place, *skels, *transfers)
    tops = from_all_groups(group_skel)

    coords, left, right = call(
        forms_body,
        [((dim, rows), BF), ((rows, 128), BF), ((128, rows), BF)],
        [VMEM] * 4,
        flops=rows * 1024,
        nbytes=rows * 128 * 8,
        name="forms",
    )(*parts)
    before = lax.ppermute(coords, "leaf", up)
    after = lax.ppermute(coords, "leaf", down)

    (leaf_field,) = call(
        leaf_field_body,
        [((4 * RANK, width), F32)],
        [VMEM] * 3,
        flops=2 * 4 * RANK * 4 * RANK * 512,
        exps=4 * RANK * 4 * RANK,
        nbytes=2 * 1024 * 1024,
        name="leaf_field",
    )(coords, leaf_skeleton, leaf_skel)

    def near_own(*args):
        return near_own_body(dim, *args)

    def near_far(*args):
        return near_far_body(dim, *args)

    tile_flops = 2 * LEAF * LEAF * 512
    (near_own_sum,) = call(
        near_own,
        [((rows, width), F32)],
        [SMEM, SMEM, SMEM, VMEM, VMEM, VMEM],
        flops=5 * tile_flops,
        exps=5 * LEAF * LEAF,
        nbytes=8 * 1024 * 1024,
        name="near_own",
    )(near_list, near_count, place, left, right, weights)

    (totals,) = call(
        top_body,
        [((width, RANK), BF)],
        [SMEM] + [VMEM] * 14,
        scratch=[pltpu.VMEM((16, RANK), BF)],
        flops=2 * LEAF * LEAF * 512 * 2,
        exps=2 * LEAF * LEAF,
        nbytes=2 * 1024 * 1024,
        name="top",
    )(place, *coord_parts, *tops, *skels, full_transfer)
    returned = [totals[:64]] + [flipped(totals[flip * 64 : (flip + 1) * 64], flip) for flip in (1, 2, 3)]

    (near_sum,) = call(
        near_far,
        [((rows, width), F32)],
        [SMEM, SMEM, SMEM] + [VMEM] * 6,
        scratch=[pltpu.VMEM((2, 128, rows), BF)],
        flops=7 * tile_flops,
        exps=7 * LEAF * LEAF,
        nbytes=12 * 1024 * 1024,
        name="near_far",
    )(near_list, near_count, place, left, before, after, w_before, w_after, near_own_sum)

    return pl.pallas_call(
        finish_body,
        grid=(4,),
        out_shape=jax.ShapeDtypeStruct((rows, width), F32),
        in_specs=[SMEM]
        + [VMEM] * 4
        + [
            pl.BlockSpec((RANK, RANK), lambda i: (0, i)),
            pl.BlockSpec((RANK, LEAF), lambda i: (i, 0)),
            pl.BlockSpec((RANK, width), lambda i: (i, 0)),
            pl.BlockSpec((LEAF, width), lambda i: (i, 0)),
        ],
        out_specs=pl.BlockSpec((LEAF, width), lambda i: (i, 0)),
        scratch_shapes=[pltpu.VMEM((width, RANK), F32)],
        cost_estimate=pl.CostEstimate(
            flops=2 * 5 * RANK * LEAF * width, transcendentals=0, bytes_accessed=10 * 1024 * 1024
        ),
        name="finish",
    )(place, *returned, dev_transfer, leaf_basis, leaf_field, near_sum)


def solution(mesh):
    in_specs = (
        P("leaf", "cols"),
        P("leaf", "cols"),
        P("leaf", None),
        P("leaf", None),
        P("leaf", None),
        P("leaf", None),
        P("leaf", None),
        P(),
        P("leaf", None),
        P("leaf"),
    )
    out_specs = P("leaf", "cols")
    return jax.shard_map(
        per_device, mesh=mesh, in_specs=in_specs, out_specs=out_specs, check_vma=False
    )
```

```python
import functools

import jax
import jax.numpy as jnp
from jax import lax
from jax.experimental import pallas as pl
from jax.experimental.pallas import tpu as pltpu
from jax.sharding import PartitionSpec as P

LEAF = 1024
RANK = 256
SHARPNESS = 2.0
LOG2E = 1.4426950408889634
BF = jnp.bfloat16
F32 = jnp.float32


VMEM = pl.BlockSpec(memory_space=pltpu.VMEM)
SMEM = pl.BlockSpec(memory_space=pltpu.SMEM)


def mm(a, b):
    return lax.dot_general(a, b, (((1,), (0,)), ((), ())), preferred_element_type=F32)


def mm_nt(a, b):
    return lax.dot_general(a, b, (((1,), (1,)), ((), ())), preferred_element_type=F32)


def mm_tn(a, b):
    return lax.dot_general(a, b, (((0,), (0,)), ((), ())), preferred_element_type=F32)


def call(body, outs, in_specs, scratch=(), flops=0, exps=0, nbytes=0, vmem=8):
    return pl.pallas_call(
        body,
        out_shape=[jax.ShapeDtypeStruct(s, d) for s, d in outs],
        in_specs=in_specs,
        out_specs=[VMEM] * len(outs),
        scratch_shapes=list(scratch),
        cost_estimate=pl.CostEstimate(flops=flops, transcendentals=exps, bytes_accessed=nbytes),
        compiler_params=pltpu.CompilerParams(vmem_limit_bytes=vmem * 1024 * 1024),
    )


def one_hot(index_row, rows):
    numbers = lax.broadcasted_iota(jnp.int32, (rows, index_row.shape[1]), 0)
    return jnp.where(numbers == index_row, 1.0, 0.0).astype(BF)


def tails(coords_t):
    wide = coords_t.astype(F32)
    half = -0.5 * jnp.sum(wide * wide, axis=0, keepdims=True)
    high = half.astype(BF).astype(F32)
    rest = half - high
    mid = rest.astype(BF).astype(F32)
    low = rest - mid
    row = lax.broadcasted_iota(jnp.int32, (16, coords_t.shape[1]), 0)

    def pieces(base, ones):
        out = jnp.where((row >= ones) & (row < ones + 3), 1.0, 0.0)
        out = jnp.where(row == base, high, out)
        out = jnp.where(row == base + 1, mid, out)
        return jnp.where(row == base + 2, low, out)

    return pieces(3, 0), pieces(0, 3)


def right_form(coords_t):
    _, tail = tails(coords_t)
    n = coords_t.shape[1]
    return jnp.concatenate([coords_t, tail.astype(BF), jnp.zeros((48, n), BF)], axis=0)


def left_form(coords_t):
    tail, _ = tails(coords_t)
    n = coords_t.shape[1]
    wide = jnp.concatenate([coords_t.astype(F32), tail, jnp.zeros((48, n), F32)], axis=0)
    return wide.T.astype(BF)


def kernel_block(left, right, dim):
    scale = 2.0 * SHARPNESS / dim * LOG2E
    return jnp.exp2(mm(left, right) * scale).astype(BF)


def column_share(position):
    return (position % 4) ^ (2 * (position // 4 % 2))


def skel_body(weights, basis, transfer, leaf_skel, nodes, weights_in, basis_in, transfer_in, sems):
    def copies(leaf):
        rows = pl.ds(leaf * LEAF, LEAF)
        ranks = pl.ds(leaf * RANK, RANK)
        return (
            pltpu.make_async_copy(basis.at[ranks], basis_in.at[ranks], sems.at[leaf]),
            pltpu.make_async_copy(weights.at[rows], weights_in.at[rows], sems.at[4 + leaf]),
        )

    whole = pltpu.make_async_copy(transfer, transfer_in, sems.at[8])
    for leaf in range(4):
        for copy in copies(leaf):
            copy.start()
        if leaf == 0:
            whole.start()
    total = None
    for leaf in range(4):
        rows = slice(leaf * RANK, (leaf + 1) * RANK)
        for copy in copies(leaf):
            copy.wait()
        skel = mm(basis_in[rows, :], weights_in[leaf * LEAF : (leaf + 1) * LEAF, :]).astype(BF)
        leaf_skel[rows, :] = skel
        if leaf == 0:
            whole.wait()
        part = mm(transfer_in[:, rows], skel)
        total = part if total is None else total + part
    nodes[...] = total.T.astype(BF)


def select_body(
    p0, p1, p2, p3, leaf_skeleton, dev_skeleton, group_skeleton, nodes, coords, leaf_coords, k0, k1, k2, k3
):
    position = lax.axis_index("leaf")
    member, group, share = position % 4, position // 4, column_share(position)
    for n, part in enumerate((p0, p1, p2, p3)):
        coords[pl.ds(n * 16, 16), :] = part[...]
    for leaf in range(4):
        hot = one_hot(leaf_skeleton[pl.ds(leaf, 1), :], LEAF)
        picked = mm(coords[:, leaf * LEAF : (leaf + 1) * LEAF], hot)
        leaf_coords[:, leaf * RANK : (leaf + 1) * RANK] = picked.astype(BF)
    node_coords = mm(leaf_coords[...], one_hot(dev_skeleton[...], 4 * RANK)).astype(BF)
    chosen = group_skeleton[pl.ds(group, 1), :] - member * RANK
    group_coords = mm(node_coords, one_hot(chosen, RANK)).astype(BF)
    for flip, out in enumerate((k0, k1, k2, k3)):
        start = pl.multiple_of((share ^ flip) * 64, 64)
        out[0:64, :] = nodes[pl.ds(start, 64), :]
        out[64:128, :] = node_coords
        out[128:192, :] = group_coords


def forms_body(coords, left, right):
    for leaf in range(4):
        cols = slice(leaf * LEAF, (leaf + 1) * LEAF)
        value = coords[:, cols]
        left[cols, :] = left_form(value)
        right[:, cols] = right_form(value)


def leaf_field_body(dim, coords, leaf_skel, field):
    picked = [coords[:, leaf * RANK : (leaf + 1) * RANK] for leaf in range(4)]
    lefts = [left_form(value) for value in picked]
    rights = [right_form(value) for value in picked]
    for i in range(4):
        total = None
        for j in range(4):
            if i != j:
                part = mm(kernel_block(lefts[i], rights[j], dim), leaf_skel[j * RANK : (j + 1) * RANK, :])
                total = part if total is None else total + part
        field[i * RANK : (i + 1) * RANK, :] = total


def near_tile(out, left, right, weights, leaf, source, opening, dim, first=0):
    cols = pl.ds(pl.multiple_of(source * LEAF, LEAF), LEAF)
    for chunk in range(4):
        rows = pl.ds(pl.multiple_of(leaf * LEAF + chunk * 256, 256), 256)
        out_rows = pl.ds(pl.multiple_of((leaf - first) * LEAF + chunk * 256, 256), 256)
        block = kernel_block(left[rows, :], right[:, cols], dim)
        part = mm(block, weights[cols, :])
        if opening:
            out[out_rows, :] = part
        else:
            out[out_rows, :] += part


def near_own_body(dim, first, near_list, near_count, left, right, weights, out):
    base = lax.axis_index("leaf") * 4

    def leaf_step(leaf, carry):
        near_tile(out, left, right, weights, leaf, leaf, True, dim, first)

        def slot_step(slot, carry):
            source = near_list[leaf, slot] - base
            active = (slot < near_count[leaf]) & (source >= 0) & (source < 4)

            @pl.when(active)
            def _():
                near_tile(out, left, right, weights, leaf, source, False, dim, first)

            return carry

        return lax.fori_loop(1, 3, slot_step, carry)

    lax.fori_loop(first, first + out.shape[0] // LEAF, leaf_step, 0)


def near_far_body(dim, near_list, near_count, left, before, after, w_up, w_down, w_late, start_a, start_b, out, right):
    position = lax.axis_index("leaf")
    base = position * 4
    low = position % 2 == 0
    up_late = low & (position % 8 != 0)
    down_late = jnp.logical_not(low) & (position % 8 != 7)
    for leaf in range(4):
        cols = slice(leaf * LEAF, (leaf + 1) * LEAF)
        right[0, :, cols] = right_form(before[:, cols])
        right[1, :, cols] = right_form(after[:, cols])
    half = start_a.shape[0]
    out[:half, :] = start_a[...]
    out[half:, :] = start_b[...]

    def leaf_step(leaf, carry):
        def slot_step(slot, carry):
            source = near_list[leaf, slot] - base
            active = slot < near_count[leaf]
            behind = active & (source < 0) & (source >= -4)
            ahead = active & (source >= 4) & (source < 8)

            @pl.when(behind & up_late)
            def _():
                near_tile(out, left, right.at[0], w_late, leaf, source + 4, False, dim)

            @pl.when(behind & jnp.logical_not(up_late))
            def _():
                near_tile(out, left, right.at[0], w_up, leaf, source + 4, False, dim)

            @pl.when(ahead & down_late)
            def _():
                near_tile(out, left, right.at[1], w_late, leaf, source - 4, False, dim)

            @pl.when(ahead & jnp.logical_not(down_late))
            def _():
                near_tile(out, left, right.at[1], w_down, leaf, source - 4, False, dim)

            return carry

        return lax.fori_loop(1, 3, slot_step, carry)

    lax.fori_loop(0, 4, leaf_step, 0)


def group_body(r0, r1, r2, r3, g0, g1, g2, g3, packed, transfer):
    member = lax.axis_index("leaf") % 4
    for flip, part in enumerate((g0, g1, g2, g3)):
        rows = pl.ds(pl.multiple_of((member ^ flip) * 64, 64), 64)
        transfer[rows, :] = part[...]
    total, coords = None, None
    for flip, part in enumerate((r0, r1, r2, r3)):
        cols = pl.ds(pl.multiple_of((member ^ flip) * RANK, RANK), RANK)
        value = mm_nt(part[0:64, :], transfer[:, cols])
        picked = part[128:192, :].astype(F32)
        total = value if total is None else total + value
        coords = picked if coords is None else coords + picked
    packed[0:64, :] = total.astype(BF)
    packed[64:128, :] = coords.astype(BF)


def top_body(dim, own, other, s1, s2, s3, s4, s5, s6, s7, r0, r1, r2, r3, transfer, *outs):
    member = lax.axis_index("leaf") % 4
    own_left = left_form(own[64:128, :])
    top = None
    blocks = [(other, 0)] + [(ref, row) for ref in (s1, s2, s3, s4, s5, s6, s7) for row in (0, 128)]
    for ref, row in blocks:
        block = kernel_block(own_left, right_form(ref[row + 64 : row + 128, :]), dim)
        part = mm_nt(ref[row : row + 64, :], block)
        top = part if top is None else top + part
    top = top.astype(BF)
    nodes = (r0, r1, r2, r3)
    lefts = [left_form(node[64:128, :]) for node in nodes]
    rights = [right_form(node[64:128, :]) for node in nodes]
    for i in range(4):
        cols = pl.ds(pl.multiple_of((member ^ i) * RANK, RANK), RANK)
        total = mm(top, transfer[:, cols])
        for j in range(4):
            if i != j:
                total = total + mm(nodes[j][0:64, :], kernel_block(lefts[j], rights[i], dim))
        outs[i][...] = total.astype(BF)


def finish_body(t0, t1, t2, t3, transfer, basis, field, near, out, total):
    leaf = pl.program_id(0)
    share = column_share(lax.axis_index("leaf"))

    @pl.when(leaf == 0)
    def _():
        for flip, part in enumerate((t0, t1, t2, t3)):
            rows = pl.ds(pl.multiple_of((share ^ flip) * 64, 64), 64)
            total[rows, :] = part[...]
        node_total = total[...].astype(F32).T.astype(BF)
        total[...] = node_total

    ranks = pl.ds(pl.multiple_of(leaf * RANK, RANK), RANK)
    rows = pl.ds(pl.multiple_of(leaf * LEAF, LEAF), LEAF)
    leaf_total = (field[ranks, :] + mm_tn(transfer[:, ranks], total[...])).astype(BF)
    out[...] = near[rows, :] + mm_tn(basis[ranks, :], leaf_total)


def per_device(
    points,
    weights,
    leaf_basis,
    dev_transfer,
    group_transfer,
    leaf_skeleton,
    dev_skeleton,
    group_skeleton,
    near_list,
    near_count,
):
    count = lax.axis_size("leaf")
    cols_count = lax.axis_size("cols")
    dim = points.shape[1] * cols_count
    width = weights.shape[1]
    rows = points.shape[0]

    def moved(value, pairs, axis="leaf"):
        return lax.ppermute(value, axis, pairs)

    def flipped(value, flip):
        return moved(value, [(i, i ^ flip) for i in range(count)])

    def shifted(value, step):
        pairs = [(i, (i + step) % cols_count) for i in range(cols_count)]
        return moved(value, pairs, "cols")

    def raised(value, step):
        return moved(value, [(i, (i + 8 * step) % count) for i in range(count)])

    up = [(i, i + 1) for i in range(count - 1)]
    down = [(j, i) for i, j in up]
    shard = points.T
    parts = [shard] + [shifted(shard, step) for step in (1, 2, 3)]
    transfer_1 = flipped(group_transfer, 1)
    transfer_2 = flipped(group_transfer, 2)
    transfer_3 = flipped(transfer_2, 1)
    transfers = [group_transfer, transfer_1, transfer_2, transfer_3]
    is_late = lambda pair: pair[1] % 8 != (0 if pair[0] < pair[1] else 7) and pair[1] % 2 == (pair[0] > pair[1])
    w_up = moved(weights, [pair for pair in up if not is_late(pair)])
    w_down = moved(weights, [pair for pair in down if not is_late(pair)])
    w_late = moved(weights, [pair for pair in up + down if is_late(pair)])

    leaf_skel, nodes = call(
        skel_body,
        [((4 * RANK, width), BF), ((width, RANK), BF)],
        [pl.BlockSpec(memory_space=pl.ANY)] * 3,
        scratch=[
            pltpu.VMEM((rows, width), BF),
            pltpu.VMEM((4 * RANK, LEAF), BF),
            pltpu.VMEM((RANK, 4 * RANK), BF),
            pltpu.SemaphoreType.DMA((9,)),
        ],
        flops=2 * 5 * RANK * LEAF * width,
        nbytes=5 * 1024 * 1024,
        vmem=58,
    )(weights, leaf_basis, dev_transfer)
    coords, leaf_coords, *packs = call(
        select_body,
        [((dim, rows), BF), ((dim, 4 * RANK), BF)] + [((192, RANK), BF)] * 4,
        [VMEM] * 8,
        flops=2 * 64 * RANK * 5 * LEAF * 4,
        nbytes=1024 * 1024,
    )(*parts, leaf_skeleton, dev_skeleton, group_skeleton, nodes)
    family = [packs[0]] + [flipped(packs[flip], flip) for flip in (1, 2, 3)]

    group_skel, full_transfer = call(
        group_body,
        [((128, RANK), BF), ((RANK, 4 * RANK), BF)],
        [VMEM] * 8,
        flops=2 * 64 * RANK * LEAF * 4,
        nbytes=1024 * 1024,
    )(*family, *transfers)
    other = moved(group_skel, [(i, i // 8 * 8 + (3 - i % 8 // 2) * 2 + i % 2) for i in range(count)])
    pair = jnp.concatenate([group_skel, other], axis=0)
    ring_u1, ring_d1 = raised(pair, 1), raised(pair, -1)
    ring_u2, ring_d2 = raised(ring_u1, 1), raised(ring_d1, -1)
    ring_u3, ring_d3 = raised(ring_u2, 1), raised(ring_d2, -1)
    ring_u4 = raised(ring_u3, 1)
    rings = (ring_u1, ring_d1, ring_u2, ring_d2, ring_u3, ring_d3, ring_u4)

    left, right = call(
        forms_body,
        [((rows, 128), BF), ((128, rows), BF)],
        [VMEM],
        flops=rows * 1024,
        nbytes=rows * 128 * 8,
        vmem=10,
    )(coords)
    before = moved(coords, up)
    after_coords = moved(coords, down)

    (leaf_field,) = call(
        functools.partial(leaf_field_body, dim),
        [((4 * RANK, width), F32)],
        [VMEM] * 2,
        flops=2 * 4 * RANK * 4 * RANK * 512,
        exps=4 * RANK * 4 * RANK,
        nbytes=2 * 1024 * 1024,
        vmem=12,
    )(leaf_coords, leaf_skel)

    tile_flops = 2 * LEAF * LEAF * 512
    near_parts = []
    for first in (0, 2):
        near_parts += call(
            functools.partial(near_own_body, dim, first),
            [((rows // 2, width), F32)],
            [SMEM, SMEM, VMEM, VMEM, VMEM],
            flops=5 * tile_flops // 2,
            exps=5 * LEAF * LEAF // 2,
            nbytes=6 * 1024 * 1024,
            vmem=16,
        )(near_list, near_count, left, right, weights)

    totals = call(
        functools.partial(top_body, dim),
        [((64, RANK), BF)] * 4,
        [VMEM] * 14,
        flops=2 * LEAF * LEAF * 512 * 2,
        exps=2 * LEAF * LEAF,
        nbytes=2 * 1024 * 1024,
        vmem=12,
    )(group_skel, other, *rings, *family, full_transfer)
    returned = [totals[0]] + [flipped(totals[flip], flip) for flip in (1, 2, 3)]

    (near_sum,) = call(
        functools.partial(near_far_body, dim),
        [((rows, width), F32)],
        [SMEM, SMEM] + [VMEM] * 8,
        scratch=[pltpu.VMEM((2, 128, rows), BF)],
        flops=7 * tile_flops,
        exps=7 * LEAF * LEAF,
        nbytes=12 * 1024 * 1024,
        vmem=24,
    )(near_list, near_count, left, before, after_coords, w_up, w_down, w_late, *near_parts)

    return pl.pallas_call(
        finish_body,
        grid=(4,),
        out_shape=jax.ShapeDtypeStruct((rows, width), F32),
        in_specs=[VMEM] * 8,
        out_specs=pl.BlockSpec((LEAF, width), lambda i: (i, 0)),
        scratch_shapes=[pltpu.VMEM((width, RANK), BF)],
        compiler_params=pltpu.CompilerParams(vmem_limit_bytes=12 * 1024 * 1024),
        cost_estimate=pl.CostEstimate(
            flops=2 * 5 * RANK * LEAF * width, transcendentals=0, bytes_accessed=10 * 1024 * 1024
        ),
        name="finish",
    )(*returned, dev_transfer, leaf_basis, leaf_field, near_sum)


def solution(mesh):
    in_specs = (
        P("leaf", "cols"),
        P("leaf", "cols"),
        P("leaf", None),
        P("leaf", None),
        P("leaf", None),
        P("leaf", None),
        P("leaf", None),
        P(),
        P("leaf", None),
        P("leaf"),
    )
    out_specs = P("leaf", "cols")
    return jax.shard_map(per_device, mesh=mesh, in_specs=in_specs, out_specs=out_specs, check_vma=False)
```

```python
import functools

import jax
import jax.numpy as jnp
from jax import lax
from jax.experimental import pallas as pl
from jax.experimental.pallas import tpu as pltpu
from jax.sharding import PartitionSpec as P

LEAF = 1024
RANK = 256
SHARPNESS = 2.0
LOG2E = 1.4426950408889634
BF = jnp.bfloat16
F32 = jnp.float32


VMEM = pl.BlockSpec(memory_space=pltpu.VMEM)
SMEM = pl.BlockSpec(memory_space=pltpu.SMEM)
HBM = pl.BlockSpec(memory_space=pltpu.HBM)


def mm(a, b):
    return lax.dot_general(a, b, (((1,), (0,)), ((), ())), preferred_element_type=F32)


def mm_nt(a, b):
    return lax.dot_general(a, b, (((1,), (1,)), ((), ())), preferred_element_type=F32)


def mm_tn(a, b):
    return lax.dot_general(a, b, (((0,), (0,)), ((), ())), preferred_element_type=F32)


def call(body, outs, in_specs, scratch=(), flops=0, exps=0, nbytes=0, vmem=8):
    return pl.pallas_call(
        body,
        out_shape=[jax.ShapeDtypeStruct(s, d) for s, d in outs],
        in_specs=in_specs,
        out_specs=[VMEM] * len(outs),
        scratch_shapes=list(scratch),
        cost_estimate=pl.CostEstimate(flops=flops, transcendentals=exps, bytes_accessed=nbytes),
        compiler_params=pltpu.CompilerParams(vmem_limit_bytes=vmem * 1024 * 1024),
    )


def one_hot(index_row, rows):
    numbers = lax.broadcasted_iota(jnp.int32, (rows, index_row.shape[1]), 0)
    return jnp.where(numbers == index_row, 1.0, 0.0).astype(BF)


def tails(coords_t):
    wide = coords_t.astype(F32)
    half = -0.5 * jnp.sum(wide * wide, axis=0, keepdims=True)
    high = half.astype(BF).astype(F32)
    rest = half - high
    mid = rest.astype(BF).astype(F32)
    low = rest - mid
    row = lax.broadcasted_iota(jnp.int32, (16, coords_t.shape[1]), 0)

    def pieces(base, ones):
        out = jnp.where((row >= ones) & (row < ones + 3), 1.0, 0.0)
        out = jnp.where(row == base, high, out)
        out = jnp.where(row == base + 1, mid, out)
        return jnp.where(row == base + 2, low, out)

    return pieces(3, 0), pieces(0, 3)


def right_form(coords_t):
    _, tail = tails(coords_t)
    n = coords_t.shape[1]
    return jnp.concatenate([coords_t, tail.astype(BF), jnp.zeros((48, n), BF)], axis=0)


def left_form(coords_t):
    tail, _ = tails(coords_t)
    n = coords_t.shape[1]
    wide = jnp.concatenate([coords_t.astype(F32), tail, jnp.zeros((48, n), F32)], axis=0)
    return wide.T.astype(BF)


def kernel_block(left, right, dim):
    scale = 2.0 * SHARPNESS / dim * LOG2E
    return jnp.exp2(mm(left, right) * scale).astype(BF)


def column_share(position):
    return (position % 4) ^ (2 * (position // 4 % 2))


def skel_body(
    weights,
    basis,
    transfer,
    leaf_skel,
    nodes,
    weights_in,
    basis_in,
    transfer_in,
    sems,
):
    def copies(leaf):
        rows = pl.ds(leaf * LEAF, LEAF)
        ranks = pl.ds(leaf * RANK, RANK)
        return (
            pltpu.make_async_copy(basis.at[ranks], basis_in.at[ranks], sems.at[leaf]),
            pltpu.make_async_copy(weights.at[rows], weights_in.at[rows], sems.at[4 + leaf]),
        )

    whole = pltpu.make_async_copy(transfer, transfer_in, sems.at[8])
    for leaf in range(4):
        for copy in copies(leaf):
            copy.start()
        if leaf == 0:
            whole.start()
    total = None
    for leaf in range(4):
        rows = slice(leaf * RANK, (leaf + 1) * RANK)
        for copy in copies(leaf):
            copy.wait()
        skel = mm(basis_in[rows, :], weights_in[leaf * LEAF : (leaf + 1) * LEAF, :]).astype(BF)
        leaf_skel[rows, :] = skel
        if leaf == 0:
            whole.wait()
        part = mm(transfer_in[:, rows], skel)
        total = part if total is None else total + part
    nodes[...] = total.T.astype(BF)


def select_body(p0, p1, p2, p3, picks, nodes, coords, leaf_coords, k0, k1, k2, k3):
    position = lax.axis_index("leaf")
    share = column_share(position)
    for n, part in enumerate((p0, p1, p2, p3)):
        coords[pl.ds(n * 16, 16), :] = part[...]
    for leaf in range(4):
        hot = one_hot(picks[leaf : leaf + 1, :], LEAF)
        picked = mm(coords[:, leaf * LEAF : (leaf + 1) * LEAF], hot)
        leaf_coords[:, leaf * RANK : (leaf + 1) * RANK] = picked.astype(BF)
    node_coords = mm(leaf_coords[...], one_hot(picks[4:5, :], 4 * RANK)).astype(BF)
    chosen = picks[pl.ds(5 + position // 4, 1), :] - (position % 4) * RANK
    group_coords = mm(node_coords, one_hot(chosen, RANK)).astype(BF)
    for flip, out in enumerate((k0, k1, k2, k3)):
        start = pl.multiple_of((share ^ flip) * 64, 64)
        out[0:64, :] = nodes[pl.ds(start, 64), :]
        out[64:128, :] = node_coords
        out[128:192, :] = group_coords


def forms_body(coords, left, right):
    for leaf in range(4):
        cols = slice(leaf * LEAF, (leaf + 1) * LEAF)
        value = coords[:, cols]
        left[cols, :] = left_form(value)
        right[:, cols] = right_form(value)


def leaf_field_body(dim, coords, leaf_skel, field):
    picked = [coords[:, leaf * RANK : (leaf + 1) * RANK] for leaf in range(4)]
    lefts = [left_form(value) for value in picked]
    rights = [right_form(value) for value in picked]
    for i in range(4):
        total = None
        for j in range(4):
            if i != j:
                part = mm(kernel_block(lefts[i], rights[j], dim), leaf_skel[j * RANK : (j + 1) * RANK, :])
                total = part if total is None else total + part
        field[i * RANK : (i + 1) * RANK, :] = total


def near_tile(out, left, right, weights, leaf, out_leaf, source, weight_leaf, dim):
    cols = pl.ds(pl.multiple_of(source * LEAF, LEAF), LEAF)
    weight_rows = pl.ds(pl.multiple_of(weight_leaf * LEAF, LEAF), LEAF)
    for chunk in range(4):
        rows = pl.ds(pl.multiple_of(leaf * LEAF + chunk * 256, 256), 256)
        out_rows = pl.ds(pl.multiple_of(out_leaf * LEAF + chunk * 256, 256), 256)
        block = kernel_block(left[rows, :], right[:, cols], dim)
        out[out_rows, :] += mm(block, weights[weight_rows, :])


def near_own_body(dim, leaf, near_list, near_count, left, right, weights, out):
    base = lax.axis_index("leaf") * 4
    out[...] = jnp.zeros_like(out)

    def slot_step(slot, carry):
        source = near_list[leaf, slot] - base
        active = (slot < near_count[leaf]) & (source >= 0) & (source < 4)

        @pl.when(active)
        def _():
            near_tile(out, left, right, weights, leaf, 0, source, source, dim)

        return carry

    lax.fori_loop(0, 3, slot_step, 0)


def near_neighbour_body(dim, inside, near_list, near_count, left, coords, *refs):
    if inside:
        weights, s0, s1, s2, s3, out, right = refs
        for leaf, start in enumerate((s0, s1, s2, s3)):
            out[leaf * LEAF : (leaf + 1) * LEAF, :] = start[...]
    else:
        weights_late, weights_cross, start, out, right, held = refs
        out[...] = start[...]
    position = lax.axis_index("leaf")
    even = position % 2 == 0
    edge = (position % 8 == 0) | (position % 8 == 7)
    first = jnp.where(even if inside else jnp.logical_not(even), position + 1, position - 1) * 4
    for leaf in range(4):
        cols = slice(leaf * LEAF, (leaf + 1) * LEAF)
        right[:, cols] = right_form(coords[:, cols])

    def leaf_step(leaf, carry):
        def slot_step(slot, carry):
            source = near_list[leaf, slot] - first
            active = (slot < near_count[leaf]) & (source >= 0) & (source < 4)

            if not inside:

                @pl.when(active & edge)
                def _():
                    held[...] = weights_cross[pl.ds(pl.multiple_of(source * LEAF, LEAF), LEAF), :]

                @pl.when(active & jnp.logical_not(edge))
                def _():
                    held[...] = weights_late[pl.ds(pl.multiple_of(source * LEAF, LEAF), LEAF), :]

            @pl.when(active)
            def _():
                if inside:
                    near_tile(out, left, right, weights, leaf, leaf, source, source, dim)
                else:
                    near_tile(out, left, right, held, leaf, leaf, source, 0, dim)

            return carry

        return lax.fori_loop(1, 3, slot_step, carry)

    lax.fori_loop(0, 4, leaf_step, 0)


def group_body(r0, r1, r2, r3, g0, g1, g2, g3, packed, transfer):
    member = lax.axis_index("leaf") % 4
    for flip, part in enumerate((g0, g1, g2, g3)):
        rows = pl.ds(pl.multiple_of((member ^ flip) * 64, 64), 64)
        transfer[rows, :] = part[...]
    total, coords = None, None
    for flip, part in enumerate((r0, r1, r2, r3)):
        cols = pl.ds(pl.multiple_of((member ^ flip) * RANK, RANK), RANK)
        value = mm_nt(part[0:64, :], transfer[:, cols])
        picked = part[128:192, :].astype(F32)
        total = value if total is None else total + value
        coords = picked if coords is None else coords + picked
    packed[0:64, :] = total.astype(BF)
    packed[64:128, :] = coords.astype(BF)


def top_part(own_left, blocks, dim, total):
    for ref, row in blocks:
        block = kernel_block(own_left, right_form(ref[row + 64 : row + 128, :]), dim)
        part = mm_nt(ref[row : row + 64, :], block)
        total = part if total is None else total + part
    return total


def top_start_body(dim, own, other, s1, s2, s3, s4, s5, s6, r0, r1, r2, r3, top, fields):
    own_left = left_form(own[64:128, :])
    blocks = [(other, 0)] + [(ref, row) for ref in (s1, s2, s3, s4, s5, s6) for row in (0, 128)]
    top[...] = top_part(own_left, blocks, dim, None)
    nodes = (r0, r1, r2, r3)
    lefts = [left_form(node[64:128, :]) for node in nodes]
    rights = [right_form(node[64:128, :]) for node in nodes]
    for i in range(4):
        total = None
        for j in range(4):
            if i != j:
                part = mm(nodes[j][0:64, :], kernel_block(lefts[j], rights[i], dim))
                total = part if total is None else total + part
        fields[i * 64 : (i + 1) * 64, :] = total


def top_body(dim, own, s7, top_start, fields, transfer, *outs):
    member = lax.axis_index("leaf") % 4
    own_left = left_form(own[64:128, :])
    top = top_part(own_left, [(s7, 0), (s7, 128)], dim, top_start[...]).astype(BF)
    for i in range(4):
        cols = pl.ds(pl.multiple_of((member ^ i) * RANK, RANK), RANK)
        outs[i][...] = (fields[i * 64 : (i + 1) * 64, :] + mm(top, transfer[:, cols])).astype(BF)


def finish_body(t0, t1, t2, t3, transfer, basis, field, near, out, total):
    leaf = pl.program_id(0)
    share = column_share(lax.axis_index("leaf"))

    @pl.when(leaf == 0)
    def _():
        for flip, part in enumerate((t0, t1, t2, t3)):
            rows = pl.ds(pl.multiple_of((share ^ flip) * 64, 64), 64)
            total[rows, :] = part[...]
        node_total = total[...].astype(F32).T.astype(BF)
        total[...] = node_total

    ranks = pl.ds(pl.multiple_of(leaf * RANK, RANK), RANK)
    rows = pl.ds(pl.multiple_of(leaf * LEAF, LEAF), LEAF)
    leaf_total = (field[ranks, :] + mm_tn(transfer[:, ranks], total[...])).astype(BF)
    out[...] = near[rows, :] + mm_tn(basis[ranks, :], leaf_total)


def per_device(
    points,
    weights,
    leaf_basis,
    dev_transfer,
    group_transfer,
    leaf_skeleton,
    dev_skeleton,
    group_skeleton,
    near_list,
    near_count,
):
    count = lax.axis_size("leaf")
    cols_count = lax.axis_size("cols")
    dim = points.shape[1] * cols_count
    width = weights.shape[1]
    rows = points.shape[0]

    def moved(value, pairs, axis="leaf"):
        return lax.ppermute(value, axis, pairs)

    def flipped(value, flip):
        return moved(value, [(i, i ^ flip) for i in range(count)])

    def shifted(value, step):
        pairs = [(i, (i + step) % cols_count) for i in range(cols_count)]
        return moved(value, pairs, "cols")

    def raised(value, step):
        return moved(value, [(i, (i + (-8 if i % 8 == 7 else 8) * step) % count) for i in range(count)])

    up = [(i, i + 1) for i in range(count - 1)]
    down = [(j, i) for i, j in up]
    picks = jnp.concatenate([leaf_skeleton, dev_skeleton, group_skeleton], axis=0)
    shard = points.T
    parts = [shard] + [shifted(shard, step) for step in (1, 2, 3)]
    transfer_1 = flipped(group_transfer, 1)
    transfer_2 = flipped(group_transfer, 2)
    transfer_3 = flipped(transfer_2, 1)
    transfers = [group_transfer, transfer_1, transfer_2, transfer_3]
    w_swap = flipped(weights, 1)
    others = [(i, j) for i, j in up if j % 2 == 0] + [(i, j) for i, j in down if j % 2 == 1]
    crossing = [(i, j) for i, j in others if i // 8 != j // 8]
    w_cross = moved(weights, crossing)
    w_late = moved(weights, [(i, j) for i, j in others if i // 8 == j // 8])

    leaf_skel, nodes = call(
        skel_body,
        [((4 * RANK, width), BF), ((width, RANK), BF)],
        [HBM] * 3,
        scratch=[
            pltpu.VMEM((rows, width), BF),
            pltpu.VMEM((4 * RANK, LEAF), BF),
            pltpu.VMEM((RANK, 4 * RANK), BF),
            pltpu.SemaphoreType.DMA((9,)),
        ],
        flops=2 * 5 * RANK * LEAF * width,
        nbytes=5 * 1024 * 1024,
        vmem=53,
    )(weights, leaf_basis, dev_transfer)
    coords, leaf_coords, *packs = call(
        select_body,
        [((dim, rows), BF), ((dim, 4 * RANK), BF)] + [((192, RANK), BF)] * 4,
        [VMEM] * 6,
        flops=2 * 64 * RANK * 5 * LEAF * 4,
        nbytes=1024 * 1024,
    )(*parts, picks, nodes)
    family = [packs[0]] + [flipped(packs[flip], flip) for flip in (1, 2, 3)]

    group_skel, full_transfer = call(
        group_body,
        [((128, RANK), BF), ((RANK, 4 * RANK), BF)],
        [VMEM] * 8,
        flops=2 * 64 * RANK * LEAF * 4,
        nbytes=1024 * 1024,
    )(*family, *transfers)
    other = moved(group_skel, [(i, i // 8 * 8 + (3 - i % 8 // 2) * 2 + i % 2) for i in range(count)])
    pair = jnp.concatenate([group_skel, other], axis=0)
    ring_u1, ring_d1 = raised(pair, 1), raised(pair, -1)
    ring_u2, ring_d2 = raised(ring_u1, 1), raised(ring_d1, -1)
    ring_u3, ring_d3 = raised(ring_u2, 1), raised(ring_d2, -1)
    ring_u4 = raised(ring_u3, 1)
    rings = (ring_u1, ring_d1, ring_u2, ring_d2, ring_u3, ring_d3, ring_u4)

    left, right = call(
        forms_body,
        [((rows, 128), BF), ((128, rows), BF)],
        [VMEM],
        flops=rows * 1024,
        nbytes=rows * 128 * 8,
        vmem=10,
    )(coords)
    inner = flipped(coords, 1)
    outer = moved(coords, others)

    (leaf_field,) = call(
        functools.partial(leaf_field_body, dim),
        [((4 * RANK, width), F32)],
        [VMEM] * 2,
        flops=2 * 4 * RANK * 4 * RANK * 512,
        exps=4 * RANK * 4 * RANK,
        nbytes=2 * 1024 * 1024,
        vmem=12,
    )(leaf_coords, leaf_skel)

    tile_flops = 2 * LEAF * LEAF * 512
    near_parts = []
    for first in range(4):
        near_parts += call(
            functools.partial(near_own_body, dim, first),
            [((LEAF, width), F32)],
            [SMEM, SMEM, VMEM, VMEM, VMEM],
            flops=3 * tile_flops // 2,
            exps=3 * LEAF * LEAF // 2,
            nbytes=6 * 1024 * 1024,
            vmem=16,
        )(near_list, near_count, left, right, weights)

    top_start, fields = call(
        functools.partial(top_start_body, dim),
        [((64, RANK), F32), ((4 * 64, RANK), F32)],
        [VMEM] * 12,
        flops=2 * LEAF * LEAF * 512 * 2,
        exps=2 * LEAF * LEAF,
        nbytes=2 * 1024 * 1024,
        vmem=12,
    )(group_skel, other, *rings[:6], *family)
    totals = call(
        functools.partial(top_body, dim),
        [((64, RANK), BF)] * 4,
        [VMEM] * 5,
        flops=2 * LEAF * LEAF * 64,
        exps=RANK * RANK * 2,
        nbytes=1024 * 1024,
    )(group_skel, rings[6], top_start, fields, full_transfer)
    returned = [totals[0]] + [flipped(totals[flip], flip) for flip in (1, 2, 3)]

    def near_neighbour(inside, *args):
        return call(
            functools.partial(near_neighbour_body, dim, inside),
            [((rows, width), F32)],
            [SMEM, SMEM] + [VMEM] * len(args),
            scratch=[pltpu.VMEM((128, rows), BF)] + [pltpu.VMEM((LEAF, width), BF)] * (not inside),
            flops=3 * tile_flops,
            exps=3 * LEAF * LEAF,
            nbytes=12 * 1024 * 1024,
            vmem=12,
        )(near_list, near_count, *args)[0]

    near_inner = near_neighbour(True, left, inner, w_swap, *near_parts)
    near_sum = near_neighbour(False, left, outer, w_late, w_cross, near_inner)

    return pl.pallas_call(
        finish_body,
        grid=(4,),
        out_shape=jax.ShapeDtypeStruct((rows, width), F32),
        in_specs=[VMEM] * 8,
        out_specs=pl.BlockSpec((LEAF, width), lambda i: (i, 0)),
        scratch_shapes=[pltpu.VMEM((width, RANK), BF)],
        compiler_params=pltpu.CompilerParams(vmem_limit_bytes=12 * 1024 * 1024),
        cost_estimate=pl.CostEstimate(
            flops=2 * 5 * RANK * LEAF * width, transcendentals=0, bytes_accessed=10 * 1024 * 1024
        ),
        name="finish",
    )(*returned, dev_transfer, leaf_basis, leaf_field, near_sum)


def solution(mesh):
    in_specs = (
        P("leaf", "cols"),
        P("leaf", "cols"),
        P("leaf", None),
        P("leaf", None),
        P("leaf", None),
        P("leaf", None),
        P("leaf", None),
        P(),
        P("leaf", None),
        P("leaf"),
    )
    out_specs = P("leaf", "cols")
    return jax.shard_map(per_device, mesh=mesh, in_specs=in_specs, out_specs=out_specs, check_vma=False)
```

```python
import functools

import jax
import jax.numpy as jnp
from jax import lax
from jax.experimental import pallas as pl
from jax.experimental.pallas import tpu as pltpu
from jax.sharding import PartitionSpec as P

LEAF = 1024
RANK = 256
SHARPNESS = 2.0
LOG2E = 1.4426950408889634
BF = jnp.bfloat16
F32 = jnp.float32


VMEM = pl.BlockSpec(memory_space=pltpu.VMEM)
SMEM = pl.BlockSpec(memory_space=pltpu.SMEM)
HBM = pl.BlockSpec(memory_space=pltpu.HBM)


def mm(a, b):
    return lax.dot_general(a, b, (((1,), (0,)), ((), ())), preferred_element_type=F32)


def mm_nt(a, b):
    return lax.dot_general(a, b, (((1,), (1,)), ((), ())), preferred_element_type=F32)


def mm_tn(a, b):
    return lax.dot_general(a, b, (((0,), (0,)), ((), ())), preferred_element_type=F32)


def call(body, outs, in_specs, scratch=(), flops=0, exps=0, nbytes=0, vmem=8):
    return pl.pallas_call(
        body,
        out_shape=[jax.ShapeDtypeStruct(s, d) for s, d in outs],
        in_specs=in_specs,
        out_specs=[VMEM] * len(outs),
        scratch_shapes=list(scratch),
        cost_estimate=pl.CostEstimate(flops=flops, transcendentals=exps, bytes_accessed=nbytes),
        compiler_params=pltpu.CompilerParams(vmem_limit_bytes=vmem * 1024 * 1024),
    )


def one_hot(index_row, rows):
    numbers = lax.broadcasted_iota(jnp.int32, (rows, index_row.shape[1]), 0)
    return jnp.where(numbers == index_row, 1.0, 0.0).astype(BF)


def tails(coords_t):
    wide = coords_t.astype(F32)
    half = -0.5 * jnp.sum(wide * wide, axis=0, keepdims=True)
    high = half.astype(BF).astype(F32)
    rest = half - high
    mid = rest.astype(BF).astype(F32)
    low = rest - mid
    row = lax.broadcasted_iota(jnp.int32, (16, coords_t.shape[1]), 0)

    def pieces(base, ones):
        out = jnp.where((row >= ones) & (row < ones + 3), 1.0, 0.0)
        out = jnp.where(row == base, high, out)
        out = jnp.where(row == base + 1, mid, out)
        return jnp.where(row == base + 2, low, out)

    return pieces(3, 0), pieces(0, 3)


def right_form(coords_t):
    _, tail = tails(coords_t)
    n = coords_t.shape[1]
    return jnp.concatenate([coords_t, tail.astype(BF), jnp.zeros((48, n), BF)], axis=0)


def left_form(coords_t):
    tail, _ = tails(coords_t)
    n = coords_t.shape[1]
    wide = jnp.concatenate([coords_t.astype(F32), tail, jnp.zeros((48, n), F32)], axis=0)
    return wide.T.astype(BF)


def kernel_block(left, right, dim):
    scale = 2.0 * SHARPNESS / dim * LOG2E
    return jnp.exp2(mm(left, right) * scale).astype(BF)


def column_share(position):
    return (position % 4) ^ (2 * (position // 4 % 2))


def skel_body(
    weights,
    basis,
    transfer,
    leaf_skel,
    nodes,
    weights_in,
    basis_in,
    transfer_in,
    sems,
):
    def copies(leaf):
        rows = pl.ds(leaf * LEAF, LEAF)
        ranks = pl.ds(leaf * RANK, RANK)
        return (
            pltpu.make_async_copy(basis.at[ranks], basis_in.at[ranks], sems.at[leaf]),
            pltpu.make_async_copy(weights.at[rows], weights_in.at[rows], sems.at[4 + leaf]),
        )

    whole = pltpu.make_async_copy(transfer, transfer_in, sems.at[8])
    for leaf in range(4):
        for copy in copies(leaf):
            copy.start()
        if leaf == 0:
            whole.start()
    total = None
    for leaf in range(4):
        rows = slice(leaf * RANK, (leaf + 1) * RANK)
        for copy in copies(leaf):
            copy.wait()
        skel = mm(basis_in[rows, :], weights_in[leaf * LEAF : (leaf + 1) * LEAF, :]).astype(BF)
        leaf_skel[rows, :] = skel
        if leaf == 0:
            whole.wait()
        part = mm(transfer_in[:, rows], skel)
        total = part if total is None else total + part
    nodes[...] = total.T.astype(BF)


def select_body(p0, p1, p2, p3, picks, nodes, coords, leaf_coords, k0, k1, k2, k3):
    position = lax.axis_index("leaf")
    share = column_share(position)
    for n, part in enumerate((p0, p1, p2, p3)):
        coords[pl.ds(n * 16, 16), :] = part[...]
    for leaf in range(4):
        hot = one_hot(picks[leaf : leaf + 1, :], LEAF)
        picked = mm(coords[:, leaf * LEAF : (leaf + 1) * LEAF], hot)
        leaf_coords[:, leaf * RANK : (leaf + 1) * RANK] = picked.astype(BF)
    node_coords = mm(leaf_coords[...], one_hot(picks[4:5, :], 4 * RANK)).astype(BF)
    chosen = picks[pl.ds(5 + position // 4, 1), :] - (position % 4) * RANK
    group_coords = mm(node_coords, one_hot(chosen, RANK)).astype(BF)
    for flip, out in enumerate((k0, k1, k2, k3)):
        start = pl.multiple_of((share ^ flip) * 64, 64)
        out[0:64, :] = nodes[pl.ds(start, 64), :]
        out[64:128, :] = node_coords
        out[128:192, :] = group_coords


def forms_body(coords, left, right):
    for leaf in range(4):
        cols = slice(leaf * LEAF, (leaf + 1) * LEAF)
        value = coords[:, cols]
        left[cols, :] = left_form(value)
        right[:, cols] = right_form(value)


def leaf_field_body(dim, coords, leaf_skel, field):
    picked = [coords[:, leaf * RANK : (leaf + 1) * RANK] for leaf in range(4)]
    lefts = [left_form(value) for value in picked]
    rights = [right_form(value) for value in picked]
    for i in range(4):
        total = None
        for j in range(4):
            if i != j:
                part = mm(kernel_block(lefts[i], rights[j], dim), leaf_skel[j * RANK : (j + 1) * RANK, :])
                total = part if total is None else total + part
        field[i * RANK : (i + 1) * RANK, :] = total


def near_tile(out, left, right, weights, leaf, out_leaf, source, weight_leaf, dim):
    cols = pl.ds(pl.multiple_of(source * LEAF, LEAF), LEAF)
    weight_rows = pl.ds(pl.multiple_of(weight_leaf * LEAF, LEAF), LEAF)
    for chunk in range(4):
        rows = pl.ds(pl.multiple_of(leaf * LEAF + chunk * 256, 256), 256)
        out_rows = pl.ds(pl.multiple_of(out_leaf * LEAF + chunk * 256, 256), 256)
        block = kernel_block(left[rows, :], right[:, cols], dim)
        out[out_rows, :] += mm(block, weights[weight_rows, :])


def near_own_body(dim, leaf, near_list, near_count, left, right, weights, out):
    base = lax.axis_index("leaf") * 4
    out[...] = jnp.zeros_like(out)

    def slot_step(slot, carry):
        source = near_list[leaf, slot] - base
        active = (slot < near_count[leaf]) & (source >= 0) & (source < 4)

        @pl.when(active)
        def _():
            near_tile(out, left, right, weights, leaf, 0, source, source, dim)

        return carry

    lax.fori_loop(0, 3, slot_step, 0)


def near_neighbour_body(dim, inside, opening, near_list, near_count, left, coords, *refs):
    if inside:
        weights, s0, s1, out, right = refs
        held = None
    else:
        weights_late, weights_cross, s0, s1, out, right, held = refs
    half = s0.shape[0]
    out[:half, :] = s0[...]
    out[half:, :] = s1[...]
    position = lax.axis_index("leaf")
    even = position % 2 == 0
    edge = (position % 8 == 0) | (position % 8 == 7)
    first = jnp.where(even if inside else jnp.logical_not(even), position + 1, position - 1) * 4
    for leaf in range(4):
        cols = slice(leaf * LEAF, (leaf + 1) * LEAF)
        right[:, cols] = right_form(coords[:, cols])

    def leaf_step(leaf, carry):
        def slot_step(slot, carry):
            source = near_list[leaf, slot] - first
            active = (slot < near_count[leaf]) & (source >= 0) & (source < 4)

            if not inside:

                @pl.when(active & edge)
                def _():
                    held[...] = weights_cross[pl.ds(pl.multiple_of(source * LEAF, LEAF), LEAF), :]

                @pl.when(active & jnp.logical_not(edge))
                def _():
                    held[...] = weights_late[pl.ds(pl.multiple_of(source * LEAF, LEAF), LEAF), :]

            @pl.when(active)
            def _():
                if inside:
                    near_tile(out, left, right, weights, leaf, leaf - opening, source, source, dim)
                else:
                    near_tile(out, left, right, held, leaf, leaf, source, 0, dim)

            return carry

        return lax.fori_loop(1, 3, slot_step, carry)

    lax.fori_loop(opening, opening + out.shape[0] // LEAF, leaf_step, 0)


def group_body(r0, r1, r2, r3, g0, g1, g2, g3, packed, transfer):
    member = lax.axis_index("leaf") % 4
    for flip, part in enumerate((g0, g1, g2, g3)):
        rows = pl.ds(pl.multiple_of((member ^ flip) * 64, 64), 64)
        transfer[rows, :] = part[...]
    total, coords = None, None
    for flip, part in enumerate((r0, r1, r2, r3)):
        cols = pl.ds(pl.multiple_of((member ^ flip) * RANK, RANK), RANK)
        value = mm_nt(part[0:64, :], transfer[:, cols])
        picked = part[128:192, :].astype(F32)
        total = value if total is None else total + value
        coords = picked if coords is None else coords + picked
    packed[0:64, :] = total.astype(BF)
    packed[64:128, :] = coords.astype(BF)


def top_part(own_left, blocks, dim, total):
    for ref, row in blocks:
        block = kernel_block(own_left, right_form(ref[row + 64 : row + 128, :]), dim)
        part = mm_nt(ref[row : row + 64, :], block)
        total = part if total is None else total + part
    return total


def top_start_body(dim, own, other, s1, s2, s3, s4, s5, s6, r0, r1, r2, r3, top, fields):
    own_left = left_form(own[64:128, :])
    blocks = [(other, 0)] + [(ref, row) for ref in (s1, s2, s3, s4, s5, s6) for row in (0, 128)]
    top[...] = top_part(own_left, blocks, dim, None)
    nodes = (r0, r1, r2, r3)
    lefts = [left_form(node[64:128, :]) for node in nodes]
    rights = [right_form(node[64:128, :]) for node in nodes]
    for i in range(4):
        total = None
        for j in range(4):
            if i != j:
                part = mm(nodes[j][0:64, :], kernel_block(lefts[j], rights[i], dim))
                total = part if total is None else total + part
        fields[i * 64 : (i + 1) * 64, :] = total


def top_body(dim, own, s7, top_start, fields, transfer, *outs):
    member = lax.axis_index("leaf") % 4
    own_left = left_form(own[64:128, :])
    top = top_part(own_left, [(s7, 0), (s7, 128)], dim, top_start[...]).astype(BF)
    for i in range(4):
        cols = pl.ds(pl.multiple_of((member ^ i) * RANK, RANK), RANK)
        outs[i][...] = (fields[i * 64 : (i + 1) * 64, :] + mm(top, transfer[:, cols])).astype(BF)


def finish_body(t0, t1, t2, t3, transfer, basis, field, near, out, total):
    leaf = pl.program_id(0)
    share = column_share(lax.axis_index("leaf"))

    @pl.when(leaf == 0)
    def _():
        for flip, part in enumerate((t0, t1, t2, t3)):
            rows = pl.ds(pl.multiple_of((share ^ flip) * 64, 64), 64)
            total[rows, :] = part[...]
        node_total = total[...].astype(F32).T.astype(BF)
        total[...] = node_total

    ranks = pl.ds(pl.multiple_of(leaf * RANK, RANK), RANK)
    rows = pl.ds(pl.multiple_of(leaf * LEAF, LEAF), LEAF)
    leaf_total = (field[ranks, :] + mm_tn(transfer[:, ranks], total[...])).astype(BF)
    out[...] = near[rows, :] + mm_tn(basis[ranks, :], leaf_total)


def per_device(
    points,
    weights,
    leaf_basis,
    dev_transfer,
    group_transfer,
    leaf_skeleton,
    dev_skeleton,
    group_skeleton,
    near_list,
    near_count,
):
    count = lax.axis_size("leaf")
    cols_count = lax.axis_size("cols")
    dim = points.shape[1] * cols_count
    width = weights.shape[1]
    rows = points.shape[0]

    def moved(value, pairs, axis="leaf"):
        return lax.ppermute(value, axis, pairs)

    def flipped(value, flip):
        return moved(value, [(i, i ^ flip) for i in range(count)])

    def shifted(value, step):
        pairs = [(i, (i + step) % cols_count) for i in range(cols_count)]
        return moved(value, pairs, "cols")

    def raised(value, step):
        return moved(value, [(i, (i + (-8 if i % 8 == 7 else 8) * step) % count) for i in range(count)])

    up = [(i, i + 1) for i in range(count - 1)]
    down = [(j, i) for i, j in up]
    shard = points.T
    parts = [shard] + [shifted(shard, step) for step in (1, 2, 3)]
    transfer_1 = flipped(group_transfer, 1)
    transfer_2 = flipped(group_transfer, 2)
    transfer_3 = flipped(transfer_2, 1)
    transfers = [group_transfer, transfer_1, transfer_2, transfer_3]
    w_swap = flipped(weights, 1)
    others = [(i, j) for i, j in up if j % 2 == 0] + [(i, j) for i, j in down if j % 2 == 1]
    crossing = [(i, j) for i, j in others if i // 8 != j // 8]
    w_cross = moved(weights, crossing)
    w_late = moved(weights, [(i, j) for i, j in others if i // 8 == j // 8])

    leaf_skel, nodes = call(
        skel_body,
        [((4 * RANK, width), BF), ((width, RANK), BF)],
        [HBM] * 3,
        scratch=[
            pltpu.VMEM((rows, width), BF),
            pltpu.VMEM((4 * RANK, LEAF), BF),
            pltpu.VMEM((RANK, 4 * RANK), BF),
            pltpu.SemaphoreType.DMA((9,)),
        ],
        flops=2 * 5 * RANK * LEAF * width,
        nbytes=5 * 1024 * 1024,
        vmem=53,
    )(weights, leaf_basis, dev_transfer)
    tables = (leaf_skeleton, dev_skeleton, group_skeleton)
    nodes, *tables = lax.optimization_barrier((nodes, *tables))
    picks = jnp.concatenate(tables, axis=0)
    coords, leaf_coords, *packs = call(
        select_body,
        [((dim, rows), BF), ((dim, 4 * RANK), BF)] + [((192, RANK), BF)] * 4,
        [VMEM] * 6,
        flops=2 * 64 * RANK * 5 * LEAF * 4,
        nbytes=1024 * 1024,
    )(*parts, picks, nodes)
    family = [packs[0]] + [flipped(packs[flip], flip) for flip in (1, 2, 3)]

    group_skel, full_transfer = call(
        group_body,
        [((128, RANK), BF), ((RANK, 4 * RANK), BF)],
        [VMEM] * 8,
        flops=2 * 64 * RANK * LEAF * 4,
        nbytes=1024 * 1024,
    )(*family, *transfers)
    other = moved(group_skel, [(i, i // 8 * 8 + (3 - i % 8 // 2) * 2 + i % 2) for i in range(count)])
    pair = jnp.concatenate([group_skel, other], axis=0)
    ring_u1, ring_d1 = raised(pair, 1), raised(pair, -1)
    ring_u2, ring_d2 = raised(ring_u1, 1), raised(ring_d1, -1)
    ring_u3, ring_d3 = raised(ring_u2, 1), raised(ring_d2, -1)
    ring_u4 = raised(ring_u3, 1)
    rings = (ring_u1, ring_d1, ring_u2, ring_d2, ring_u3, ring_d3, ring_u4)

    left, right = call(
        forms_body,
        [((rows, 128), BF), ((128, rows), BF)],
        [VMEM],
        flops=rows * 1024,
        nbytes=rows * 128 * 8,
        vmem=10,
    )(coords)
    inner = flipped(coords, 1)
    outer = moved(coords, others)

    (leaf_field,) = call(
        functools.partial(leaf_field_body, dim),
        [((4 * RANK, width), F32)],
        [VMEM] * 2,
        flops=2 * 4 * RANK * 4 * RANK * 512,
        exps=4 * RANK * 4 * RANK,
        nbytes=2 * 1024 * 1024,
        vmem=12,
    )(leaf_coords, leaf_skel)

    tile_flops = 2 * LEAF * LEAF * 512
    near_parts = []
    for first in range(4):
        near_parts += call(
            functools.partial(near_own_body, dim, first),
            [((LEAF, width), F32)],
            [SMEM, SMEM, VMEM, VMEM, VMEM],
            flops=3 * tile_flops // 2,
            exps=3 * LEAF * LEAF // 2,
            nbytes=6 * 1024 * 1024,
            vmem=16,
        )(near_list, near_count, left, right, weights)

    top_start, fields = call(
        functools.partial(top_start_body, dim),
        [((64, RANK), F32), ((4 * 64, RANK), F32)],
        [VMEM] * 12,
        flops=2 * LEAF * LEAF * 512 * 2,
        exps=2 * LEAF * LEAF,
        nbytes=2 * 1024 * 1024,
        vmem=12,
    )(group_skel, other, *rings[:6], *family)
    totals = call(
        functools.partial(top_body, dim),
        [((64, RANK), BF)] * 4,
        [VMEM] * 5,
        flops=2 * LEAF * LEAF * 64,
        exps=RANK * RANK * 2,
        nbytes=1024 * 1024,
    )(group_skel, rings[6], top_start, fields, full_transfer)
    returned = [totals[0]] + [flipped(totals[flip], flip) for flip in (1, 2, 3)]

    def near_neighbour(inside, opening, *args):
        return call(
            functools.partial(near_neighbour_body, dim, inside, opening),
            [((2 * args[-1].shape[0], width), F32)],
            [SMEM, SMEM] + [VMEM] * len(args),
            scratch=[pltpu.VMEM((128, rows), BF)] + [pltpu.VMEM((LEAF, width), BF)] * (not inside),
            flops=3 * tile_flops,
            exps=3 * LEAF * LEAF,
            nbytes=12 * 1024 * 1024,
            vmem=12,
        )(near_list, near_count, *args)[0]

    halves = [
        near_neighbour(True, n, left, inner, w_swap, near_parts[n], near_parts[n + 1]) for n in (0, 2)
    ]
    near_sum = near_neighbour(False, 0, left, outer, w_late, w_cross, *halves)

    return pl.pallas_call(
        finish_body,
        grid=(4,),
        out_shape=jax.ShapeDtypeStruct((rows, width), F32),
        in_specs=[VMEM] * 8,
        out_specs=pl.BlockSpec((LEAF, width), lambda i: (i, 0)),
        scratch_shapes=[pltpu.VMEM((width, RANK), BF)],
        compiler_params=pltpu.CompilerParams(vmem_limit_bytes=12 * 1024 * 1024),
        cost_estimate=pl.CostEstimate(
            flops=2 * 5 * RANK * LEAF * width, transcendentals=0, bytes_accessed=10 * 1024 * 1024
        ),
        name="finish",
    )(*returned, dev_transfer, leaf_basis, leaf_field, near_sum)


def solution(mesh):
    in_specs = (
        P("leaf", "cols"),
        P("leaf", "cols"),
        P("leaf", None),
        P("leaf", None),
        P("leaf", None),
        P("leaf", None),
        P("leaf", None),
        P(),
        P("leaf", None),
        P("leaf"),
    )
    out_specs = P("leaf", "cols")
    return jax.shard_map(per_device, mesh=mesh, in_specs=in_specs, out_specs=out_specs, check_vma=False)
```

```python
import functools

import jax
import jax.numpy as jnp
from jax import lax
from jax.experimental import pallas as pl
from jax.experimental.pallas import tpu as pltpu
from jax.sharding import PartitionSpec as P

LEAF = 1024
ROWS, COLS = "leaf", "cols"
RANK = 256
SHARPNESS = 2.0
LOG2E = 1.4426950408889634
BF = jnp.bfloat16
F32 = jnp.float32


VMEM = pl.BlockSpec(memory_space=pltpu.VMEM)
SMEM = pl.BlockSpec(memory_space=pltpu.SMEM)
HBM = pl.BlockSpec(memory_space=pltpu.HBM)


def mm(a, b):
    return lax.dot_general(a, b, (((1,), (0,)), ((), ())), preferred_element_type=F32)


def mm_nt(a, b):
    return lax.dot_general(a, b, (((1,), (1,)), ((), ())), preferred_element_type=F32)


def mm_tn(a, b):
    return lax.dot_general(a, b, (((0,), (0,)), ((), ())), preferred_element_type=F32)


def call(body, outs, in_specs, scratch=(), flops=0, exps=0, nbytes=0, vmem=8):
    kernel = pl.pallas_call(
        body,
        out_shape=[jax.ShapeDtypeStruct(s, d) for s, d in outs],
        in_specs=in_specs,
        out_specs=[VMEM] * len(outs),
        scratch_shapes=list(scratch),
        cost_estimate=pl.CostEstimate(flops=flops, transcendentals=exps, bytes_accessed=nbytes),
        compiler_params=pltpu.CompilerParams(vmem_limit_bytes=vmem * 1024 * 1024),
    )
    return kernel


def one_hot(index_row, rows):
    numbers = lax.broadcasted_iota(jnp.int32, (rows, index_row.shape[1]), 0)
    return jnp.where(numbers == index_row, 1.0, 0.0).astype(BF)


def tails(coords_t):
    wide = coords_t.astype(F32)
    half = -0.5 * jnp.sum(wide * wide, axis=0, keepdims=True)
    high = half.astype(BF).astype(F32)
    rest = half - high
    mid = rest.astype(BF).astype(F32)
    low = rest - mid
    row = lax.broadcasted_iota(jnp.int32, (16, coords_t.shape[1]), 0)

    def pieces(base, ones):
        out = jnp.where((row >= ones) & (row < ones + 3), 1.0, 0.0)
        out = jnp.where(row == base, high, out)
        out = jnp.where(row == base + 1, mid, out)
        return jnp.where(row == base + 2, low, out)

    return pieces(3, 0), pieces(0, 3)


def right_form(coords_t):
    _, tail = tails(coords_t)
    n = coords_t.shape[1]
    return jnp.concatenate([coords_t, tail.astype(BF), jnp.zeros((48, n), BF)], axis=0)


def left_form(coords_t):
    tail, _ = tails(coords_t)
    n = coords_t.shape[1]
    wide = jnp.concatenate([coords_t.astype(F32), tail, jnp.zeros((48, n), F32)], axis=0)
    return wide.T.astype(BF)


def kernel_block(left, right, dim):
    scale = 2.0 * SHARPNESS / dim * LOG2E
    return jnp.exp2(mm(left, right) * scale).astype(BF)


def column_share(position):
    return (position % 4) ^ (2 * (position // 4 % 2))


def skel_body(
    weights,
    basis,
    transfer,
    leaf_skel,
    nodes,
    weights_in,
    basis_in,
    transfer_in,
    sems,
):
    def copies(leaf):
        rows = pl.ds(leaf * LEAF, LEAF)
        ranks = pl.ds(leaf * RANK, RANK)
        return (
            pltpu.make_async_copy(basis.at[ranks], basis_in.at[ranks], sems.at[leaf]),
            pltpu.make_async_copy(weights.at[rows], weights_in.at[rows], sems.at[4 + leaf]),
        )

    whole = pltpu.make_async_copy(transfer, transfer_in, sems.at[8])
    for leaf in range(4):
        for copy in copies(leaf):
            copy.start()
        if leaf == 0:
            whole.start()
    total = None
    for leaf in range(4):
        rows = slice(leaf * RANK, (leaf + 1) * RANK)
        for copy in copies(leaf):
            copy.wait()
        skel = mm(basis_in[rows, :], weights_in[leaf * LEAF : (leaf + 1) * LEAF, :]).astype(BF)
        leaf_skel[rows, :] = skel
        if leaf == 0:
            whole.wait()
        part = mm(transfer_in[:, rows], skel)
        total = part if total is None else total + part
    nodes[...] = total.T.astype(BF)


def select_body(p0, p1, p2, p3, picks, nodes, coords, leaf_coords, k0, k1, k2, k3):
    position = lax.axis_index(ROWS)
    share = column_share(position)
    for n, part in enumerate((p0, p1, p2, p3)):
        coords[pl.ds(n * 16, 16), :] = part[...]
    for leaf in range(4):
        hot = one_hot(picks[leaf : leaf + 1, :], LEAF)
        picked = mm(coords[:, leaf * LEAF : (leaf + 1) * LEAF], hot)
        leaf_coords[:, leaf * RANK : (leaf + 1) * RANK] = picked.astype(BF)
    node_coords = mm(leaf_coords[...], one_hot(picks[4:5, :], 4 * RANK)).astype(BF)
    chosen = picks[pl.ds(5 + position // 4, 1), :] - (position % 4) * RANK
    group_coords = mm(node_coords, one_hot(chosen, RANK)).astype(BF)
    for flip, out in enumerate((k0, k1, k2, k3)):
        start = pl.multiple_of((share ^ flip) * 64, 64)
        out[0:64, :] = nodes[pl.ds(start, 64), :]
        out[64:128, :] = node_coords
        out[128:192, :] = group_coords


def forms_body(coords, left, right):
    for leaf in range(4):
        cols = slice(leaf * LEAF, (leaf + 1) * LEAF)
        value = coords[:, cols]
        left[cols, :] = left_form(value)
        right[:, cols] = right_form(value)


def leaf_field_body(dim, coords, leaf_skel, field):
    picked = [coords[:, leaf * RANK : (leaf + 1) * RANK] for leaf in range(4)]
    lefts = [left_form(value) for value in picked]
    rights = [right_form(value) for value in picked]
    for i in range(4):
        total = None
        for j in range(4):
            if i != j:
                part = mm(kernel_block(lefts[i], rights[j], dim), leaf_skel[j * RANK : (j + 1) * RANK, :])
                total = part if total is None else total + part
        field[i * RANK : (i + 1) * RANK, :] = total


def near_tile(out, left, right, weights, leaf, out_leaf, source, weight_leaf, dim):
    cols = pl.ds(pl.multiple_of(source * LEAF, LEAF), LEAF)
    weight_rows = pl.ds(pl.multiple_of(weight_leaf * LEAF, LEAF), LEAF)
    for chunk in range(4):
        rows = pl.ds(pl.multiple_of(leaf * LEAF + chunk * 256, 256), 256)
        out_rows = pl.ds(pl.multiple_of(out_leaf * LEAF + chunk * 256, 256), 256)
        block = kernel_block(left[rows, :], right[:, cols], dim)
        out[out_rows, :] += mm(block, weights[weight_rows, :])


def near_own_body(dim, leaf, near_list, near_count, left, right, weights, out):
    base = lax.axis_index(ROWS) * 4
    out[...] = jnp.zeros_like(out)

    def slot_step(slot, carry):
        source = near_list[leaf, slot] - base
        active = (slot < near_count[leaf]) & (source >= 0) & (source < 4)

        @pl.when(active)
        def _():
            near_tile(out, left, right, weights, leaf, 0, source, source, dim)

        return carry

    lax.fori_loop(0, 3, slot_step, 0)


def near_neighbour_body(dim, inside, opening, near_list, near_count, left, coords, *refs):
    if inside:
        weights, s0, s1, out, right = refs
        held = None
    else:
        weights_late, weights_cross, s0, s1, out, right, held = refs
    half = s0.shape[0]
    out[:half, :] = s0[...]
    out[half:, :] = s1[...]
    position = lax.axis_index(ROWS)
    even = position % 2 == 0
    edge = (position % 8 == 0) | (position % 8 == 7)
    first = jnp.where(even if inside else jnp.logical_not(even), position + 1, position - 1) * 4
    for leaf in range(4):
        cols = slice(leaf * LEAF, (leaf + 1) * LEAF)
        right[:, cols] = right_form(coords[:, cols])

    def leaf_step(leaf, carry):
        def slot_step(slot, carry):
            source = near_list[leaf, slot] - first
            active = (slot < near_count[leaf]) & (source >= 0) & (source < 4)

            if not inside:

                @pl.when(active & edge)
                def _():
                    held[...] = weights_cross[pl.ds(pl.multiple_of(source * LEAF, LEAF), LEAF), :]

                @pl.when(active & jnp.logical_not(edge))
                def _():
                    held[...] = weights_late[pl.ds(pl.multiple_of(source * LEAF, LEAF), LEAF), :]

            @pl.when(active)
            def _():
                if inside:
                    near_tile(out, left, right, weights, leaf, leaf - opening, source, source, dim)
                else:
                    near_tile(out, left, right, held, leaf, leaf, source, 0, dim)

            return carry

        return lax.fori_loop(1, 3, slot_step, carry)

    lax.fori_loop(opening, opening + out.shape[0] // LEAF, leaf_step, 0)


def group_body(r0, r1, r2, r3, g0, g1, g2, g3, packed, transfer):
    member = lax.axis_index(ROWS) % 4
    for flip, part in enumerate((g0, g1, g2, g3)):
        rows = pl.ds(pl.multiple_of((member ^ flip) * 64, 64), 64)
        transfer[rows, :] = part[...]
    total, coords = None, None
    for flip, part in enumerate((r0, r1, r2, r3)):
        cols = pl.ds(pl.multiple_of((member ^ flip) * RANK, RANK), RANK)
        value = mm_nt(part[0:64, :], transfer[:, cols])
        picked = part[128:192, :].astype(F32)
        total = value if total is None else total + value
        coords = picked if coords is None else coords + picked
    packed[0:64, :] = total.astype(BF)
    packed[64:128, :] = coords.astype(BF)


def top_part(own_left, blocks, dim, total):
    for ref, row in blocks:
        block = kernel_block(own_left, right_form(ref[row + 64 : row + 128, :]), dim)
        part = mm_nt(ref[row : row + 64, :], block)
        total = part if total is None else total + part
    return total


def top_start_body(dim, own, other, s1, s2, s3, s4, s5, s6, r0, r1, r2, r3, top, fields):
    own_left = left_form(own[64:128, :])
    blocks = [(other, 0)] + [(ref, row) for ref in (s1, s2, s3, s4, s5, s6) for row in (0, 128)]
    top[...] = top_part(own_left, blocks, dim, None)
    nodes = (r0, r1, r2, r3)
    lefts = [left_form(node[64:128, :]) for node in nodes]
    rights = [right_form(node[64:128, :]) for node in nodes]
    for i in range(4):
        total = None
        for j in range(4):
            if i != j:
                part = mm(nodes[j][0:64, :], kernel_block(lefts[j], rights[i], dim))
                total = part if total is None else total + part
        fields[i * 64 : (i + 1) * 64, :] = total


def top_body(dim, own, s7, top_start, fields, transfer, *outs):
    member = lax.axis_index(ROWS) % 4
    own_left = left_form(own[64:128, :])
    top = top_part(own_left, [(s7, 0), (s7, 128)], dim, top_start[...]).astype(BF)
    for i in range(4):
        cols = pl.ds(pl.multiple_of((member ^ i) * RANK, RANK), RANK)
        outs[i][...] = (fields[i * 64 : (i + 1) * 64, :] + mm(top, transfer[:, cols])).astype(BF)


def finish_body(t0, t1, t2, t3, transfer, basis, field, near, out, total):
    leaf = pl.program_id(0)
    share = column_share(lax.axis_index(ROWS))

    @pl.when(leaf == 0)
    def _():
        for flip, part in enumerate((t0, t1, t2, t3)):
            rows = pl.ds(pl.multiple_of((share ^ flip) * 64, 64), 64)
            total[rows, :] = part[...]
        node_total = total[...].astype(F32).T.astype(BF)
        total[...] = node_total

    ranks = pl.ds(pl.multiple_of(leaf * RANK, RANK), RANK)
    rows = pl.ds(pl.multiple_of(leaf * LEAF, LEAF), LEAF)
    leaf_total = (field[ranks, :] + mm_tn(transfer[:, ranks], total[...])).astype(BF)
    out[...] = near[rows, :] + mm_tn(basis[ranks, :], leaf_total)


def per_device(
    points,
    weights,
    leaf_basis,
    dev_transfer,
    group_transfer,
    leaf_skeleton,
    dev_skeleton,
    group_skeleton,
    near_list,
    near_count,
):
    count = lax.axis_size(ROWS)
    cols_count = lax.axis_size(COLS)
    dim = points.shape[1] * cols_count
    width = weights.shape[1]
    rows = points.shape[0]

    def moved(value, pairs, axis=ROWS):
        return lax.ppermute(value, axis, pairs)

    def flipped(value, flip):
        return moved(value, [(i, i ^ flip) for i in range(count)])

    def shifted(value, step):
        pairs = [(i, (i + step) % cols_count) for i in range(cols_count)]
        return moved(value, pairs, COLS)

    def raised(value, step):
        return moved(value, [(i, (i + (-8 if i % 8 == 7 else 8) * step) % count) for i in range(count)])

    up = [(i, i + 1) for i in range(count - 1)]
    down = [(j, i) for i, j in up]
    shard = points.T
    parts = [shard] + [shifted(shard, step) for step in (1, 2, 3)]
    transfer_1 = flipped(group_transfer, 1)
    transfer_2 = flipped(group_transfer, 2)
    transfer_3 = flipped(transfer_2, 1)
    transfers = [group_transfer, transfer_1, transfer_2, transfer_3]
    w_swap = flipped(weights, 1)
    others = [(i, j) for i, j in up if j % 2 == 0] + [(i, j) for i, j in down if j % 2 == 1]
    crossing = [(i, j) for i, j in others if i // 8 != j // 8]
    w_cross = moved(weights, crossing)
    w_late = moved(weights, [(i, j) for i, j in others if i // 8 == j // 8])

    leaf_skel, nodes = call(
        skel_body,
        [((4 * RANK, width), BF), ((width, RANK), BF)],
        [HBM] * 3,
        scratch=[
            pltpu.VMEM((rows, width), BF),
            pltpu.VMEM((4 * RANK, LEAF), BF),
            pltpu.VMEM((RANK, 4 * RANK), BF),
            pltpu.SemaphoreType.DMA((9,)),
        ],
        flops=2 * 5 * RANK * LEAF * width,
        nbytes=5 * 1024 * 1024,
        vmem=53,
    )(weights, leaf_basis, dev_transfer)
    tables = (leaf_skeleton, dev_skeleton, group_skeleton)
    nodes, *tables = lax.optimization_barrier((nodes, *tables))
    picks = jnp.concatenate(tables, axis=0)
    coords, leaf_coords, *packs = call(
        select_body,
        [((dim, rows), BF), ((dim, 4 * RANK), BF)] + [((192, RANK), BF)] * 4,
        [VMEM] * 6,
        flops=2 * 64 * RANK * 5 * LEAF * 4,
        nbytes=1024 * 1024,
    )(*parts, picks, nodes)
    family = [packs[0]] + [flipped(packs[flip], flip) for flip in (1, 2, 3)]

    group_skel, full_transfer = call(
        group_body,
        [((128, RANK), BF), ((RANK, 4 * RANK), BF)],
        [VMEM] * 8,
        flops=2 * 64 * RANK * LEAF * 4,
        nbytes=1024 * 1024,
    )(*family, *transfers)
    other = moved(group_skel, [(i, i // 8 * 8 + (3 - i % 8 // 2) * 2 + i % 2) for i in range(count)])
    pair = jnp.concatenate([group_skel, other], axis=0)
    ring_u1, ring_d1 = raised(pair, 1), raised(pair, -1)
    ring_u2, ring_d2 = raised(ring_u1, 1), raised(ring_d1, -1)
    ring_u3, ring_d3 = raised(ring_u2, 1), raised(ring_d2, -1)
    ring_u4 = raised(ring_u3, 1)
    rings = (ring_u1, ring_d1, ring_u2, ring_d2, ring_u3, ring_d3, ring_u4)

    left, right = call(
        forms_body,
        [((rows, 128), BF), ((128, rows), BF)],
        [VMEM],
        flops=rows * 1024,
        nbytes=rows * 128 * 8,
        vmem=10,
    )(coords)
    inner = flipped(coords, 1)
    outer = moved(coords, others)

    (leaf_field,) = call(
        functools.partial(leaf_field_body, dim),
        [((4 * RANK, width), F32)],
        [VMEM] * 2,
        flops=2 * 4 * RANK * 4 * RANK * 512,
        exps=4 * RANK * 4 * RANK,
        nbytes=2 * 1024 * 1024,
        vmem=12,
    )(leaf_coords, leaf_skel)

    tile_flops = 2 * LEAF * LEAF * 512
    near_parts = []
    for first in range(4):
        near_parts += call(
            functools.partial(near_own_body, dim, first),
            [((LEAF, width), F32)],
            [SMEM, SMEM, VMEM, VMEM, VMEM],
            flops=3 * tile_flops // 2,
            exps=3 * LEAF * LEAF // 2,
            nbytes=6 * 1024 * 1024,
            vmem=16,
        )(near_list, near_count, left, right, weights)

    top_start, fields = call(
        functools.partial(top_start_body, dim),
        [((64, RANK), F32), ((4 * 64, RANK), F32)],
        [VMEM] * 12,
        flops=2 * LEAF * LEAF * 512 * 2,
        exps=2 * LEAF * LEAF,
        nbytes=2 * 1024 * 1024,
        vmem=12,
    )(group_skel, other, *rings[:6], *family)
    totals = call(
        functools.partial(top_body, dim),
        [((64, RANK), BF)] * 4,
        [VMEM] * 5,
        flops=2 * LEAF * LEAF * 64,
        exps=RANK * RANK * 2,
        nbytes=1024 * 1024,
    )(group_skel, rings[6], top_start, fields, full_transfer)
    returned = [totals[0]] + [flipped(totals[flip], flip) for flip in (1, 2, 3)]

    def near_neighbour(inside, opening, *args):
        return call(
            functools.partial(near_neighbour_body, dim, inside, opening),
            [((2 * args[-1].shape[0], width), F32)],
            [SMEM, SMEM] + [VMEM] * len(args),
            scratch=[pltpu.VMEM((128, rows), BF)] + [pltpu.VMEM((LEAF, width), BF)] * (not inside),
            flops=3 * tile_flops,
            exps=3 * LEAF * LEAF,
            nbytes=12 * 1024 * 1024,
            vmem=12,
        )(near_list, near_count, *args)[0]

    halves = [
        near_neighbour(True, n, left, inner, w_swap, near_parts[n], near_parts[n + 1]) for n in (0, 2)
    ]
    near_sum = near_neighbour(False, 0, left, outer, w_late, w_cross, *halves)

    return pl.pallas_call(
        finish_body,
        grid=(4,),
        out_shape=jax.ShapeDtypeStruct((rows, width), F32),
        in_specs=[VMEM] * 8,
        out_specs=pl.BlockSpec((LEAF, width), lambda i: (i, 0)),
        scratch_shapes=[pltpu.VMEM((width, RANK), BF)],
        compiler_params=pltpu.CompilerParams(vmem_limit_bytes=12 * 1024 * 1024),
        cost_estimate=pl.CostEstimate(
            flops=2 * 5 * RANK * LEAF * width, transcendentals=0, bytes_accessed=10 * 1024 * 1024
        ),
    )(*returned, dev_transfer, leaf_basis, leaf_field, near_sum)


def solution(mesh):
    in_specs = (
        P(ROWS, COLS),
        P(ROWS, COLS),
        P(ROWS, None),
        P(ROWS, None),
        P(ROWS, None),
        P(ROWS, None),
        P(ROWS, None),
        P(),
        P(ROWS, None),
        P(ROWS),
    )
    out_specs = P(ROWS, COLS)
    return jax.shard_map(per_device, mesh=mesh, in_specs=in_specs, out_specs=out_specs, check_vma=False)
```

```python
import functools

import jax
import jax.numpy as jnp
from jax import lax
from jax.experimental import pallas as pl
from jax.experimental.pallas import tpu as pltpu
from jax.sharding import PartitionSpec as P

LEAF = 1024
ROWS, COLS = "leaf", "cols"
RANK = 256
SHARPNESS = 2.0
LOG2E = 1.4426950408889634
BF = jnp.bfloat16
F32 = jnp.float32


VMEM = pl.BlockSpec(memory_space=pltpu.VMEM)
SMEM = pl.BlockSpec(memory_space=pltpu.SMEM)
HBM = pl.BlockSpec(memory_space=pltpu.HBM)


def mm(a, b):
    return lax.dot_general(a, b, (((1,), (0,)), ((), ())), preferred_element_type=F32)


def mm_nt(a, b):
    return lax.dot_general(a, b, (((1,), (1,)), ((), ())), preferred_element_type=F32)


def call(body, outs, in_specs, scratch=(), flops=0, exps=0, nbytes=0, vmem=8):
    kernel = pl.pallas_call(
        body,
        out_shape=[jax.ShapeDtypeStruct(s, d) for s, d in outs],
        in_specs=in_specs,
        out_specs=[VMEM] * len(outs),
        scratch_shapes=list(scratch),
        cost_estimate=pl.CostEstimate(flops=flops, transcendentals=exps, bytes_accessed=nbytes),
        compiler_params=pltpu.CompilerParams(vmem_limit_bytes=vmem * 1024 * 1024),
    )
    return kernel


def one_hot(index_row, rows):
    numbers = lax.broadcasted_iota(jnp.int32, (rows, index_row.shape[1]), 0)
    return jnp.where(numbers == index_row, 1.0, 0.0).astype(BF)


def tails(coords_t):
    wide = coords_t.astype(F32)
    half = -0.5 * jnp.sum(wide * wide, axis=0, keepdims=True)
    high = half.astype(BF).astype(F32)
    rest = half - high
    mid = rest.astype(BF).astype(F32)
    low = rest - mid
    row = lax.broadcasted_iota(jnp.int32, (16, coords_t.shape[1]), 0)

    def pieces(base, ones):
        out = jnp.where((row >= ones) & (row < ones + 3), 1.0, 0.0)
        out = jnp.where(row == base, high, out)
        out = jnp.where(row == base + 1, mid, out)
        return jnp.where(row == base + 2, low, out)

    return pieces(3, 0), pieces(0, 3)


def right_form(coords_t):
    _, tail = tails(coords_t)
    n = coords_t.shape[1]
    return jnp.concatenate([coords_t, tail.astype(BF), jnp.zeros((48, n), BF)], axis=0)


def left_form(coords_t):
    tail, _ = tails(coords_t)
    n = coords_t.shape[1]
    wide = jnp.concatenate([coords_t.astype(F32), tail, jnp.zeros((48, n), F32)], axis=0)
    return wide.T.astype(BF)


def kernel_block(left, right, dim):
    scale = 2.0 * SHARPNESS / dim * LOG2E
    return jnp.exp2(mm(left, right) * scale).astype(BF)


def column_share(position):
    return (position % 4) ^ (2 * (position // 4 % 2))


def skel_body(
    weights,
    basis,
    transfer,
    leaf_skel,
    nodes,
    weights_in,
    basis_in,
    transfer_in,
    sems,
):
    def copies(leaf):
        rows = pl.ds(leaf * LEAF, LEAF)
        ranks = pl.ds(leaf * RANK, RANK)
        return (
            pltpu.make_async_copy(basis.at[ranks], basis_in.at[ranks], sems.at[leaf]),
            pltpu.make_async_copy(weights.at[rows], weights_in.at[rows], sems.at[4 + leaf]),
        )

    whole = pltpu.make_async_copy(transfer, transfer_in, sems.at[8])
    for leaf in range(4):
        for copy in copies(leaf):
            copy.start()
        if leaf == 0:
            whole.start()
    total = None
    for leaf in range(4):
        rows = slice(leaf * RANK, (leaf + 1) * RANK)
        for copy in copies(leaf):
            copy.wait()
        skel = mm(basis_in[rows, :], weights_in[leaf * LEAF : (leaf + 1) * LEAF, :]).astype(BF)
        leaf_skel[rows, :] = skel
        if leaf == 0:
            whole.wait()
        part = mm(transfer_in[:, rows], skel)
        total = part if total is None else total + part
    nodes[...] = total.T.astype(BF)


def select_body(p0, p1, p2, p3, picks, nodes, coords, leaf_coords, k0, k1, k2, k3):
    position = lax.axis_index(ROWS)
    share = column_share(position)
    for n, part in enumerate((p0, p1, p2, p3)):
        coords[pl.ds(n * 16, 16), :] = part[...]
    for leaf in range(4):
        hot = one_hot(picks[leaf : leaf + 1, :], LEAF)
        picked = mm(coords[:, leaf * LEAF : (leaf + 1) * LEAF], hot)
        leaf_coords[:, leaf * RANK : (leaf + 1) * RANK] = picked.astype(BF)
    node_coords = mm(leaf_coords[...], one_hot(picks[4:5, :], 4 * RANK)).astype(BF)
    chosen = picks[pl.ds(5 + position // 4, 1), :] - (position % 4) * RANK
    group_coords = mm(node_coords, one_hot(chosen, RANK)).astype(BF)
    for flip, out in enumerate((k0, k1, k2, k3)):
        start = pl.multiple_of((share ^ flip) * 64, 64)
        out[0:64, :] = nodes[pl.ds(start, 64), :]
        out[64:128, :] = node_coords
        out[128:192, :] = group_coords


def forms_body(coords, left, right):
    for leaf in range(4):
        cols = slice(leaf * LEAF, (leaf + 1) * LEAF)
        value = coords[:, cols]
        left[cols, :] = left_form(value)
        right[:, cols] = right_form(value)


def leaf_field_body(dim, coords, leaf_skel, field):
    picked = [coords[:, leaf * RANK : (leaf + 1) * RANK] for leaf in range(4)]
    lefts = [left_form(value) for value in picked]
    rights = [right_form(value) for value in picked]
    for i in range(4):
        total = None
        for j in range(4):
            if i != j:
                part = mm(kernel_block(lefts[i], rights[j], dim), leaf_skel[j * RANK : (j + 1) * RANK, :])
                total = part if total is None else total + part
        field[i * RANK : (i + 1) * RANK, :] = total


def near_tile(out, left, right, weights, leaf, out_leaf, source, weight_leaf, dim):
    cols = pl.ds(pl.multiple_of(source * LEAF, LEAF), LEAF)
    weight_rows = pl.ds(pl.multiple_of(weight_leaf * LEAF, LEAF), LEAF)
    for chunk in range(4):
        rows = pl.ds(pl.multiple_of(leaf * LEAF + chunk * 256, 256), 256)
        out_rows = pl.ds(pl.multiple_of(out_leaf * LEAF + chunk * 256, 256), 256)
        block = kernel_block(left[rows, :], right[:, cols], dim)
        out[out_rows, :] += mm(block, weights[weight_rows, :])


def near_own_body(dim, leaf, near_list, near_count, left, right, weights, out):
    base = lax.axis_index(ROWS) * 4
    out[...] = jnp.zeros_like(out)

    def slot_step(slot, carry):
        source = near_list[leaf, slot] - base
        active = (slot < near_count[leaf]) & (source >= 0) & (source < 4)

        @pl.when(active)
        def _():
            near_tile(out, left, right, weights, leaf, 0, source, source, dim)

        return carry

    lax.fori_loop(0, 3, slot_step, 0)


def near_neighbour_body(dim, inside, opening, near_list, near_count, left, coords, *refs):
    if inside:
        weights, s0, s1, out, right = refs
        held = None
    else:
        weights_late, weights_cross, s0, s1, out, right, held = refs
    half = s0.shape[0]
    out[:half, :] = s0[...]
    out[half:, :] = s1[...]
    position = lax.axis_index(ROWS)
    even = position % 2 == 0
    edge = (position % 8 == 0) | (position % 8 == 7)
    first = jnp.where(even if inside else jnp.logical_not(even), position + 1, position - 1) * 4
    for leaf in range(4):
        cols = slice(leaf * LEAF, (leaf + 1) * LEAF)
        right[:, cols] = right_form(coords[:, cols])

    def leaf_step(leaf, carry):
        def slot_step(slot, carry):
            source = near_list[leaf, slot] - first
            active = (slot < near_count[leaf]) & (source >= 0) & (source < 4)

            if not inside:

                @pl.when(active & edge)
                def _():
                    held[...] = weights_cross[pl.ds(pl.multiple_of(source * LEAF, LEAF), LEAF), :]

                @pl.when(active & jnp.logical_not(edge))
                def _():
                    held[...] = weights_late[pl.ds(pl.multiple_of(source * LEAF, LEAF), LEAF), :]

            @pl.when(active)
            def _():
                if inside:
                    near_tile(out, left, right, weights, leaf, leaf - opening, source, source, dim)
                else:
                    near_tile(out, left, right, held, leaf, leaf, source, 0, dim)

            return carry

        return lax.fori_loop(1, 3, slot_step, carry)

    lax.fori_loop(opening, opening + out.shape[0] // LEAF, leaf_step, 0)


def group_body(r0, r1, r2, r3, g0, g1, g2, g3, packed, transfer):
    member = lax.axis_index(ROWS) % 4
    for flip, part in enumerate((g0, g1, g2, g3)):
        rows = pl.ds(pl.multiple_of((member ^ flip) * 64, 64), 64)
        transfer[rows, :] = part[...]
    total, coords = None, None
    for flip, part in enumerate((r0, r1, r2, r3)):
        cols = pl.ds(pl.multiple_of((member ^ flip) * RANK, RANK), RANK)
        value = mm_nt(part[0:64, :], transfer[:, cols])
        picked = part[128:192, :].astype(F32)
        total = value if total is None else total + value
        coords = picked if coords is None else coords + picked
    packed[0:64, :] = total.astype(BF)
    packed[64:128, :] = coords.astype(BF)


def top_part(own_left, blocks, dim, total):
    for ref, row in blocks:
        block = kernel_block(own_left, right_form(ref[row + 64 : row + 128, :]), dim)
        part = mm_nt(ref[row : row + 64, :], block)
        total = part if total is None else total + part
    return total


def top_start_body(dim, own, other, s1, s2, s3, s4, s5, s6, r0, r1, r2, r3, top, fields):
    own_left = left_form(own[64:128, :])
    blocks = [(other, 0)] + [(ref, row) for ref in (s1, s2, s3, s4, s5, s6) for row in (0, 128)]
    top[...] = top_part(own_left, blocks, dim, None)
    nodes = (r0, r1, r2, r3)
    lefts = [left_form(node[64:128, :]) for node in nodes]
    rights = [right_form(node[64:128, :]) for node in nodes]
    for i in range(4):
        total = None
        for j in range(4):
            if i != j:
                part = mm(nodes[j][0:64, :], kernel_block(lefts[j], rights[i], dim))
                total = part if total is None else total + part
        fields[i * 64 : (i + 1) * 64, :] = total


def top_body(dim, own, s7, top_start, fields, transfer, *outs):
    member = lax.axis_index(ROWS) % 4
    own_left = left_form(own[64:128, :])
    top = top_part(own_left, [(s7, 0), (s7, 128)], dim, top_start[...]).astype(BF)
    for i in range(4):
        cols = pl.ds(pl.multiple_of((member ^ i) * RANK, RANK), RANK)
        outs[i][...] = (fields[i * 64 : (i + 1) * 64, :] + mm(top, transfer[:, cols])).astype(BF)


def flip_body(transfer, basis, transfer_t, basis_t):
    transfer_t[...] = transfer[...].T
    for leaf in range(4):
        basis_t[leaf * LEAF : (leaf + 1) * LEAF, :] = basis[leaf * RANK : (leaf + 1) * RANK, :].T


def finish_body(t0, t1, t2, t3, transfer_t, basis_t, field, near, out, total):
    leaf = pl.program_id(0)
    share = column_share(lax.axis_index(ROWS))

    @pl.when(leaf == 0)
    def _():
        for flip, part in enumerate((t0, t1, t2, t3)):
            rows = pl.ds(pl.multiple_of((share ^ flip) * 64, 64), 64)
            total[rows, :] = part[...]
        node_total = total[...].astype(F32).T.astype(BF)
        total[...] = node_total

    ranks = pl.ds(pl.multiple_of(leaf * RANK, RANK), RANK)
    rows = pl.ds(pl.multiple_of(leaf * LEAF, LEAF), LEAF)
    leaf_total = (field[ranks, :] + mm(transfer_t[ranks, :], total[...])).astype(BF)
    out[...] = near[rows, :] + mm(basis_t[rows, :], leaf_total)


def per_device(
    points,
    weights,
    leaf_basis,
    dev_transfer,
    group_transfer,
    leaf_skeleton,
    dev_skeleton,
    group_skeleton,
    near_list,
    near_count,
):
    count = lax.axis_size(ROWS)
    cols_count = lax.axis_size(COLS)
    dim = points.shape[1] * cols_count
    width = weights.shape[1]
    rows = points.shape[0]

    def moved(value, pairs, axis=ROWS):
        return lax.ppermute(value, axis, pairs)

    def flipped(value, flip):
        return moved(value, [(i, i ^ flip) for i in range(count)])

    def shifted(value, step):
        pairs = [(i, (i + step) % cols_count) for i in range(cols_count)]
        return moved(value, pairs, COLS)

    def raised(value, step):
        return moved(value, [(i, (i + (-8 if i % 8 == 7 else 8) * step) % count) for i in range(count)])

    up = [(i, i + 1) for i in range(count - 1)]
    down = [(j, i) for i, j in up]
    shard = points.T
    parts = [shard] + [shifted(shard, step) for step in (1, 2, 3)]
    transfer_1 = flipped(group_transfer, 1)
    transfer_2 = flipped(group_transfer, 2)
    transfer_3 = flipped(transfer_2, 1)
    transfers = [group_transfer, transfer_1, transfer_2, transfer_3]
    w_swap = flipped(weights, 1)
    others = [(i, j) for i, j in up if j % 2 == 0] + [(i, j) for i, j in down if j % 2 == 1]
    crossing = [(i, j) for i, j in others if i // 8 != j // 8]
    w_cross = moved(weights, crossing)
    w_late = moved(weights, [(i, j) for i, j in others if i // 8 == j // 8])

    leaf_skel, nodes = call(
        skel_body,
        [((4 * RANK, width), BF), ((width, RANK), BF)],
        [HBM] * 3,
        scratch=[
            pltpu.VMEM((rows, width), BF),
            pltpu.VMEM((4 * RANK, LEAF), BF),
            pltpu.VMEM((RANK, 4 * RANK), BF),
            pltpu.SemaphoreType.DMA((9,)),
        ],
        flops=2 * 5 * RANK * LEAF * width,
        nbytes=5 * 1024 * 1024,
        vmem=53,
    )(weights, leaf_basis, dev_transfer)
    tables = (leaf_skeleton, dev_skeleton, group_skeleton)
    nodes, *tables = lax.optimization_barrier((nodes, *tables))
    picks = jnp.concatenate(tables, axis=0)
    coords, leaf_coords, *packs = call(
        select_body,
        [((dim, rows), BF), ((dim, 4 * RANK), BF)] + [((192, RANK), BF)] * 4,
        [VMEM] * 6,
        flops=2 * 64 * RANK * 5 * LEAF * 4,
        nbytes=1024 * 1024,
    )(*parts, picks, nodes)
    family = [packs[0]] + [flipped(packs[flip], flip) for flip in (1, 2, 3)]

    group_skel, full_transfer = call(
        group_body,
        [((128, RANK), BF), ((RANK, 4 * RANK), BF)],
        [VMEM] * 8,
        flops=2 * 64 * RANK * LEAF * 4,
        nbytes=1024 * 1024,
    )(*family, *transfers)
    other = moved(group_skel, [(i, i // 8 * 8 + (3 - i % 8 // 2) * 2 + i % 2) for i in range(count)])
    pair = jnp.concatenate([group_skel, other], axis=0)
    ring_u1, ring_d1 = raised(pair, 1), raised(pair, -1)
    ring_u2, ring_d2 = raised(ring_u1, 1), raised(ring_d1, -1)
    ring_u3, ring_d3 = raised(ring_u2, 1), raised(ring_d2, -1)
    ring_u4 = raised(ring_u3, 1)
    rings = (ring_u1, ring_d1, ring_u2, ring_d2, ring_u3, ring_d3, ring_u4)

    left, right = call(
        forms_body,
        [((rows, 128), BF), ((128, rows), BF)],
        [VMEM],
        flops=rows * 1024,
        nbytes=rows * 128 * 8,
        vmem=10,
    )(coords)
    inner = flipped(coords, 1)
    outer = moved(coords, others)

    (leaf_field,) = call(
        functools.partial(leaf_field_body, dim),
        [((4 * RANK, width), F32)],
        [VMEM] * 2,
        flops=2 * 4 * RANK * 4 * RANK * 512,
        exps=4 * RANK * 4 * RANK,
        nbytes=2 * 1024 * 1024,
        vmem=12,
    )(leaf_coords, leaf_skel)

    tile_flops = 2 * LEAF * LEAF * 512
    near_parts = []
    for first in range(4):
        near_parts += call(
            functools.partial(near_own_body, dim, first),
            [((LEAF, width), F32)],
            [SMEM, SMEM, VMEM, VMEM, VMEM],
            flops=3 * tile_flops // 2,
            exps=3 * LEAF * LEAF // 2,
            nbytes=6 * 1024 * 1024,
            vmem=16,
        )(near_list, near_count, left, right, weights)

    top_start, fields = call(
        functools.partial(top_start_body, dim),
        [((64, RANK), F32), ((4 * 64, RANK), F32)],
        [VMEM] * 12,
        flops=2 * LEAF * LEAF * 512 * 2,
        exps=2 * LEAF * LEAF,
        nbytes=2 * 1024 * 1024,
        vmem=12,
    )(group_skel, other, *rings[:6], *family)
    totals = call(
        functools.partial(top_body, dim),
        [((64, RANK), BF)] * 4,
        [VMEM] * 5,
        flops=2 * LEAF * LEAF * 64,
        exps=RANK * RANK * 2,
        nbytes=1024 * 1024,
    )(group_skel, rings[6], top_start, fields, full_transfer)
    returned = [totals[0]] + [flipped(totals[flip], flip) for flip in (1, 2, 3)]

    transfer_t, basis_t = call(
        flip_body,
        [((4 * RANK, RANK), BF), ((rows, RANK), BF)],
        [VMEM] * 2,
        flops=rows * RANK,
        nbytes=5 * 1024 * 1024,
    )(dev_transfer, leaf_basis)

    def near_neighbour(inside, opening, *args):
        return call(
            functools.partial(near_neighbour_body, dim, inside, opening),
            [((2 * args[-1].shape[0], width), F32)],
            [SMEM, SMEM] + [VMEM] * len(args),
            scratch=[pltpu.VMEM((128, rows), BF)] + [pltpu.VMEM((LEAF, width), BF)] * (not inside),
            flops=3 * tile_flops,
            exps=3 * LEAF * LEAF,
            nbytes=12 * 1024 * 1024,
            vmem=12,
        )(near_list, near_count, *args)[0]

    halves = [
        near_neighbour(True, n, left, inner, w_swap, near_parts[n], near_parts[n + 1]) for n in (0, 2)
    ]
    near_sum = near_neighbour(False, 0, left, outer, w_late, w_cross, *halves)

    return pl.pallas_call(
        finish_body,
        grid=(4,),
        out_shape=jax.ShapeDtypeStruct((rows, width), F32),
        in_specs=[VMEM] * 8,
        out_specs=pl.BlockSpec((LEAF, width), lambda i: (i, 0)),
        scratch_shapes=[pltpu.VMEM((width, RANK), BF)],
        compiler_params=pltpu.CompilerParams(vmem_limit_bytes=12 * 1024 * 1024),
        cost_estimate=pl.CostEstimate(
            flops=2 * 5 * RANK * LEAF * width, transcendentals=0, bytes_accessed=10 * 1024 * 1024
        ),
    )(*returned, transfer_t, basis_t, leaf_field, near_sum)


def solution(mesh):
    in_specs = (
        P(ROWS, COLS),
        P(ROWS, COLS),
        P(ROWS, None),
        P(ROWS, None),
        P(ROWS, None),
        P(ROWS, None),
        P(ROWS, None),
        P(),
        P(ROWS, None),
        P(ROWS),
    )
    out_specs = P(ROWS, COLS)
    return jax.shard_map(per_device, mesh=mesh, in_specs=in_specs, out_specs=out_specs, check_vma=False)
```
